32 devices in a mesh: band: 2 (over y), tm: 4 (over z), rows: 4 (over x, core).
Axes of the slice: x: 2, y: 2, z: 4, core: 2. Of those that a mesh axis runs over, the one named last changes fastest.
Arguments:
- recording: bfloat16 [4096, 64, 512], P('tm', ('band', 'rows')), parts along dimension 1, may hold values from -3 to 3
- traces: bfloat16 [128, 4096], P('band', 'tm'), parts along dimension 0, as said below
- footprints: float32 [64, 64, 512], P(None, ('band', 'rows')), parts along dimension 1, may hold values from 0 to 1
- correlation: float32 [64, 512], P(('band', 'rows')), parts along dimension 0, may hold values from 0.5 to 1
- support: int32 [128, 4], P('band'), parts along dimension 0, may hold values from 0 to 7, all different within a row
Outputs:
- renewed: float32 [64, 64, 512], P(None, ('band', 'rows')), parts along dimension 1
The draws below stay inside these ranges and needn't reach their ends.
There are 2 independent parts, one for each index of `band`. The reference program is written for one: setup_inputs(seed, part) draws one part's arguments, and reference() takes and returns one part's arrays. A program takes and returns all parts, laid end to end along the dimension named above; each array names one. Nothing has to cross between parts.
Inputs may be any that keep to these rules, and one draw needn't show every extreme that they name: traces are nonzero reals of magnitude at most 32 / sqrt(4096). `support`: each component names 4 different row tiles; every tile is named by some component.
All inputs are finite; a program needn't handle non-finite values.
Results may differ from the reference program's by a relative error of at most 0.0003.
Values sent between devices are 32-bit elements; how exact they have to be, the bound alone decides.
No kernel may reach another device: no remote copies, remote signals or barrier semaphores. Data moves between devices by JAX's collectives and lax.ppermute only.
A program may use at most 64 MiB of HBM per device.

```python
import math
import jax
import jax.numpy as jnp
from jax import lax

K = 64
COLS = 512
TILE = 4
SUPPORT = 4
PASSES = 4
FRAMES = 4096
ROWS = 32
NTILES = 8


def draw_traces(key, part):
    key_amp = jax.random.fold_in(key, 11)
    key_flicker = jax.random.fold_in(key, 12)
    key_noise = jax.random.fold_in(key, 13)
    amplitude = jnp.exp(jax.random.uniform(key_amp, (K, 1), jnp.float32, math.log(0.5), math.log(2.0)))
    flicker = jnp.exp(jax.random.uniform(key_flicker, (1, FRAMES), jnp.float32, 0.0, math.log(4.0)))
    bleaching = jnp.exp(-math.log(3.0) * jnp.arange(FRAMES, dtype=jnp.float32) / FRAMES)[None, :]
    activity = jnp.clip(jax.random.normal(key_noise, (K, FRAMES), jnp.float32), -4.0, 4.0)
    values = amplitude * flicker * bleaching * activity / math.sqrt(FRAMES)
    return values.astype(jnp.bfloat16)


def block_levels(stream_key, dims, split, least, high):
    level = 1.0
    for dim, shards_of in split:
        steps = jax.random.uniform(jax.random.fold_in(jax.random.fold_in(stream_key, 6), dim), (shards_of,), jnp.float32, least / len(split), high / len(split))
        level = level * jnp.repeat(jnp.exp(steps), dims[dim] // shards_of).reshape((-1,) + (1,) * (len(dims) - 1 - dim))
    return level


def picks_of(own_key, rows, number_of, top, lift):
    ranking = jax.random.permutation(jax.random.fold_in(own_key, 1), number_of)
    favour = ranking
    for power in range(3):
        favour = favour * favour // number_of
    favour = favour * lift // number_of
    chance = jax.random.randint(jax.random.fold_in(own_key, 2), (rows, number_of), 0, 4096) + favour
    fixed_rows = jax.random.permutation(jax.random.fold_in(own_key, 3), rows)[jnp.arange(number_of) % rows]
    chance = jnp.where(jnp.arange(rows)[:, None] == fixed_rows[None, :], 1 << 14, chance)
    merit = chance * number_of + jnp.arange(number_of)
    return lax.top_k(merit.astype(jnp.int32), top)[1].astype(jnp.int32)


def bell_draw(key, dims, width, reach, cuts=(), kind=jnp.bfloat16):
    result = jax.random.normal(key, dims, jnp.float32) * width
    if len(cuts) > 0:
        result = block_levels(key, dims, cuts, -0.22, 0.18) * result
    return jnp.clip(result, min=-reach, max=reach).astype(kind)


def setup_inputs(seed: int = 0, part: int = 0) -> dict:
    streams_of = jax.random.split(jax.random.key(seed), 6)
    part_splits = jax.random.split(jax.random.fold_in(streams_of[5], part), 6)
    return {
        "recording": bell_draw(part_splits[0], (FRAMES, ROWS, COLS), 0.5, 3.0, ((0, 4), (1, 4))),
        "traces": draw_traces(jax.random.fold_in(jax.random.fold_in(streams_of[5], part), 71), part),
        "footprints": jnp.clip(1.0 * jax.random.uniform(part_splits[2], (K, ROWS, COLS), jnp.float32) ** block_levels(part_splits[2], (K, ROWS, COLS), ((1, 4),), -0.2, 0.2), 0.0, 1.0),
        "correlation": jnp.clip(0.5 + 0.5 * jax.random.uniform(part_splits[3], (ROWS, COLS), jnp.float32) ** block_levels(part_splits[3], (ROWS, COLS), ((0, 4),), -0.2, 0.2), 0.5, 1.0),
        "support": picks_of(part_splits[4], K, NTILES, SUPPORT, 0),
    }


diffusion_rate = 0.24
step_scale = 0.5
epsilon = 1e-6


def relax_once(center, above, below, weight):
    side_pad = jnp.pad(center, ((0, 0), (0, 0), (1, 1)))
    beside_all = above + below + side_pad[:, :, 2:] + side_pad[:, :, :-2]
    return center + diffusion_rate * weight * (beside_all - 4.0 * center)


def reference(recording, traces, footprints, correlation, support):
    frame_count = recording.shape[0]
    row_total = footprints.shape[1]
    flattened = recording.reshape(frame_count, -1)
    gram_matrix = jnp.dot(traces, traces.T, preferred_element_type=jnp.float32)
    projected = jnp.dot(traces, flattened, preferred_element_type=jnp.float32)
    tile_ids = jnp.arange(row_total, dtype=jnp.int32) // TILE
    support_mask = jnp.any(support[:, :, None] == tile_ids[None, None, :], axis=1).astype(jnp.float32)
    all_flat = footprints.reshape(K, -1)
    gradient = jnp.dot(gram_matrix, all_flat, precision=lax.Precision.HIGHEST, preferred_element_type=jnp.float32) - projected
    updated = all_flat - step_scale * gradient / (jnp.diagonal(gram_matrix)[:, None] + epsilon)
    field = jnp.maximum(updated, 0.0).reshape(footprints.shape) * support_mask[:, :, None]
    for pass_index in range(PASSES):
        padded = jnp.pad(field, ((0, 0), (1, 1), (0, 0)))
        field = relax_once(field, padded[:, :-2], padded[:, 2:], correlation[None])
    return field * support_mask[:, :, None]
```

```python
import jax
import jax.numpy as jnp
from jax import lax
from jax.sharding import PartitionSpec as P
from jax.experimental import pallas as pl
from jax.experimental.pallas import tpu as pltpu

TILE = 4
PASSES = 4
diffusion_rate = 0.24
step_scale = 0.5
epsilon = 1e-06
TIME_BLOCK = 256
LANES = 128
HIGHEST = lax.Precision.HIGHEST


def barrier(*arrays):
    return lax.optimization_barrier(arrays)


def project_kernel(traces_ref, movie_ref, *refs):
    *out_refs, spread_ref, wide_ref, total_ref, gram_ref = refs
    comps, frames = traces_ref.shape
    rows = movie_ref.shape[0] // frames
    step = pl.program_id(0)

    @pl.when(step == 0)
    def _():
        frame = lax.broadcasted_iota(jnp.int32, spread_ref.shape, 0)
        lane = lax.broadcasted_iota(jnp.int32, spread_ref.shape, 1)
        spread_ref[...] = jnp.where(frame == lane // rows, 1.0, 0.0).astype(jnp.bfloat16)

    traces = traces_ref[...]
    repeated = jnp.dot(traces, spread_ref[...], preferred_element_type=jnp.float32).astype(jnp.bfloat16)
    phase = lax.broadcasted_iota(jnp.int32, repeated.shape, 1) % rows
    for row in range(rows):
        wide_ref[row * comps : (row + 1) * comps, :] = jnp.where(
            phase == row, repeated, jnp.zeros_like(repeated)
        )
    part = jnp.dot(wide_ref[...], movie_ref[...], preferred_element_type=jnp.float32)
    gram = lax.dot_general(traces, traces, (((1,), (1,)), ((), ())), preferred_element_type=jnp.float32)

    @pl.when(step == 0)
    def _():
        total_ref[...] = part
        gram_ref[...] = gram

    @pl.when(step > 0)
    def _():
        total_ref[...] += part
        gram_ref[...] += gram

    @pl.when(step == pl.num_programs(0) - 1)
    def _():
        for row in range(rows):
            out_refs[row][0:comps, :] = total_ref[row * comps : (row + 1) * comps, :]
        band = comps * LANES // movie_ref.shape[1] // 2
        for half in range(2):
            ref = out_refs[half]
            ref[comps:, :] = jnp.zeros((band, ref.shape[1]), jnp.float32)
            for part_index in range(ref.shape[1] // LANES):
                first = (2 * part_index + half) * band
                ref[comps:, part_index * LANES : part_index * LANES + comps] = gram_ref[first : first + band, :]


def project(traces, recording):
    frames, rows, cols = recording.shape
    comps = traces.shape[0]
    band = comps * LANES // cols // 2
    heights = [comps + (band if row < 2 else 0) for row in range(rows)]
    return pl.pallas_call(
        project_kernel,
        name="project",
        grid=(frames // TIME_BLOCK,),
        in_specs=[
            pl.BlockSpec((comps, TIME_BLOCK), lambda i: (0, i)),
            pl.BlockSpec((TIME_BLOCK * rows, cols), lambda i: (i, 0)),
        ],
        out_specs=[pl.BlockSpec((height, cols), lambda i: (0, 0)) for height in heights],
        out_shape=[jax.ShapeDtypeStruct((height, cols), jnp.float32) for height in heights],
        scratch_shapes=[
            pltpu.VMEM((TIME_BLOCK, TIME_BLOCK * rows), jnp.bfloat16),
            pltpu.VMEM((rows * comps, TIME_BLOCK * rows), jnp.bfloat16),
            pltpu.VMEM((rows * comps, cols), jnp.float32),
            pltpu.VMEM((comps, comps), jnp.float32),
        ],
        compiler_params=pltpu.CompilerParams(
            vmem_limit_bytes=58 << 20, dimension_semantics=("arbitrary",)
        ),
    )(traces, recording.reshape(frames * rows, cols))


def tiles_of(array):
    comps, rows, cols = array.shape
    pieces = array.reshape(comps, rows, cols // LANES, LANES).transpose(0, 2, 1, 3)
    return pieces.reshape(comps * rows * cols // LANES, LANES)


def from_tiles(tiles, comps, rows, cols):
    pieces = tiles.reshape(comps, cols // LANES, rows, LANES).transpose(0, 2, 1, 3)
    return pieces.reshape(comps, rows, cols)


def descend_kernel(where_ref, support_ref, footprints_ref, *refs):
    *sum_refs, out_ref = refs
    comps, cols = out_ref.shape[1:]
    rows = out_ref.shape[0]
    swapped = where_ref[1] == 1
    band = sum_refs[0].shape[0] - comps
    pairs = [
        tuple(
            jnp.where(swapped, sum_refs[2 * chunk + 1 - half][...], sum_refs[2 * chunk + half][...])
            for half in range(2)
        )
        for chunk in range(rows // 2)
    ]
    gram = jnp.concatenate(
        [
            pairs[0][half][comps:, part * LANES : part * LANES + comps]
            for part in range(cols // LANES)
            for half in range(2)
        ],
        axis=0,
    )
    own = lax.broadcasted_iota(jnp.int32, gram.shape, 0) == lax.broadcasted_iota(jnp.int32, gram.shape, 1)
    diagonal = jnp.sum(jnp.where(own, gram, 0.0), axis=1, keepdims=True)
    rate = step_scale / (diagonal + epsilon)
    for row in range(rows):
        tile = (where_ref[0] * rows + row) // TILE
        mask = jnp.max(jnp.where(support_ref[...] == tile, 1.0, 0.0), axis=1, keepdims=True)
        field = jnp.concatenate(
            [
                footprints_ref[pl.ds(piece * rows + row, comps, stride=rows * cols // LANES), :]
                for piece in range(cols // LANES)
            ],
            axis=1,
        )
        gradient = (
            jnp.dot(gram, field, precision=HIGHEST, preferred_element_type=jnp.float32)
            - pairs[row // 2][row % 2][0:comps]
        )
        out_ref[row] = jnp.maximum(field - rate * gradient, 0.0) * mask


def descend(where, support, footprints, sums):
    comps, rows, cols = footprints.shape
    return pl.pallas_call(
        descend_kernel,
        name="descend",
        in_specs=[pl.BlockSpec(memory_space=pltpu.SMEM)] + [pl.BlockSpec(memory_space=pltpu.VMEM)] * (2 + len(sums)),
        out_specs=pl.BlockSpec(memory_space=pltpu.VMEM),
        out_shape=jax.ShapeDtypeStruct((rows, comps, cols), jnp.float32),
        compiler_params=pltpu.CompilerParams(vmem_limit_bytes=40 << 20),
    )(where, support, tiles_of(footprints), *sums)


def diffuse_kernel(where_ref, support_ref, correlation_ref, field_ref, inner_ref, outer_ref, out_ref):
    rows, group, cols = field_ref.shape
    index, last = where_ref[0], where_ref[2]
    even = index % 2 == 0
    has_above = jnp.where(index > 0, 1.0, 0.0)
    has_below = jnp.where(index < last, 1.0, 0.0)
    planes = [
        jnp.where(even, outer_ref[row], inner_ref[row]) * has_above for row in range(PASSES)
    ]
    planes += [field_ref[row] for row in range(rows)]
    planes += [
        jnp.where(even, inner_ref[row], outer_ref[row]) * has_below for row in range(PASSES)
    ]
    lane = lax.broadcasted_iota(jnp.int32, (group, cols), 1)
    for pass_index in range(PASSES):
        renewed = []
        for row in range(1, len(planes) - 1):
            center = planes[row]
            left = jnp.where(lane == 0, 0.0, pltpu.roll(center, 1, 1))
            right = jnp.where(lane == cols - 1, 0.0, pltpu.roll(center, cols - 1, 1))
            weight = diffusion_rate * correlation_ref[row + pass_index : row + pass_index + 1, :]
            beside = planes[row - 1] + planes[row + 1] + left + right
            renewed.append(center + weight * (beside - 4.0 * center))
        planes = renewed
    for row in range(rows):
        tile = (index * rows + row) // TILE
        mask = jnp.max(jnp.where(support_ref[...] == tile, 1.0, 0.0), axis=1, keepdims=True)
        masked = planes[row] * mask
        for piece in range(cols // LANES):
            out_ref[pl.ds(piece * rows + row, group, stride=rows * cols // LANES), :] = masked[
                :, piece * LANES : (piece + 1) * LANES
            ]


def diffuse(where, support, correlation, field, inner, outer):
    rows, comps, cols = field.shape
    group = 8
    return pl.pallas_call(
        diffuse_kernel,
        name="diffuse",
        grid=(comps // group,),
        in_specs=[
            pl.BlockSpec(memory_space=pltpu.SMEM),
            pl.BlockSpec((group, support.shape[1]), lambda i: (i, 0)),
            pl.BlockSpec(correlation.shape, lambda i: (0, 0)),
            pl.BlockSpec((rows, group, cols), lambda i: (0, i, 0)),
            pl.BlockSpec((PASSES, group, cols), lambda i: (0, i, 0)),
            pl.BlockSpec((PASSES, group, cols), lambda i: (0, i, 0)),
        ],
        out_specs=pl.BlockSpec((group * rows * cols // LANES, LANES), lambda i: (i, 0)),
        out_shape=jax.ShapeDtypeStruct((comps * rows * cols // LANES, LANES), jnp.float32),
        compiler_params=pltpu.CompilerParams(
            vmem_limit_bytes=40 << 20, dimension_semantics=("arbitrary",)
        ),
    )(where, support, correlation, field, inner, outer)


def pairs_of(count, first):
    table = list(range(count))
    for i in range(first, count - 1, 2):
        table[i], table[i + 1] = i + 1, i
    return list(enumerate(table))


def total_over_frames(parts, odd):
    count = lax.axis_size("tm")
    sums = []
    if count != 4:
        for low, high in zip(parts[::2], parts[1::2]):
            low, high = lax.psum((low, high), "tm")
            sums += [jnp.where(odd, high, low), jnp.where(odd, low, high)]
        return sums
    near, far = pairs_of(4, 0), [(0, 3), (1, 2), (2, 1), (3, 0)]
    firsts = []
    for low, high in zip(parts[::2], parts[1::2]):
        mine, other = barrier(jnp.where(odd, high, low), jnp.where(odd, low, high))
        firsts.append((mine, lax.ppermute(other, "tm", near)))
    for mine, received in firsts:
        (received,) = barrier(received)
        (half,) = barrier(mine + received)
        (across,) = barrier(lax.ppermute(half, "tm", far))
        (whole,) = barrier(half + across)
        sums += [whole, lax.ppermute(whole, "tm", near)]
    return sums


def per_device(recording, traces, footprints, correlation, support):
    comps, rows, cols = footprints.shape
    index = lax.axis_index("rows")
    count = lax.axis_size("rows")
    part = lax.axis_index("tm")
    odd = (part == 1) | (part == 2)
    where = jnp.stack([index, odd.astype(jnp.int32), jnp.int32(count - 1)]).astype(jnp.int32)
    inside, outside = pairs_of(count, 0), pairs_of(count, 1)
    even = index % 2 == 0

    near = lax.ppermute(correlation, "rows", inside)
    away = lax.ppermute(correlation, "rows", outside)
    above, below = jnp.where(even, away, near), jnp.where(even, near, away)
    above = jnp.where(index > 0, above[rows - PASSES :], 0.0)
    below = jnp.where(index < count - 1, below[:PASSES], 0.0)
    weights = jnp.concatenate([above, correlation, below], axis=0)

    parts = project(traces, recording)
    sums = total_over_frames(parts, odd)
    stepped = descend(where, support, footprints, sums)
    top, bottom = stepped[:PASSES], stepped[rows - PASSES :]
    to_inner, to_outer = barrier(jnp.where(even, bottom, top), jnp.where(even, top, bottom))
    inner = lax.ppermute(to_inner, "rows", inside)
    outer = lax.ppermute(to_outer, "rows", outside)
    result = diffuse(where, support, weights, stepped, inner, outer)
    return from_tiles(result, comps, rows, cols)


def solution(mesh):
    return jax.shard_map(
        per_device,
        mesh=mesh,
        in_specs=(
            P("tm", ("band", "rows"), None),
            P("band", "tm"),
            P(None, ("band", "rows"), None),
            P(("band", "rows"), None),
            P("band", None),
        ),
        out_specs=P(None, ("band", "rows"), None),
        check_vma=False,
    )
```

```python
import functools

import jax
import jax.numpy as jnp
from jax import lax
from jax.sharding import PartitionSpec as P
from jax.experimental import pallas as pl
from jax.experimental.pallas import tpu as pltpu

TILE = 4
PASSES = 4
diffusion_rate = 0.24
step_scale = 0.5
epsilon = 1e-06
FRAME_BLOCK = 128
LANES = 128
GROUP = 8
TERMS = 3
HIGHEST = lax.Precision.HIGHEST
VMEM = pltpu.VMEM
WHOLE = pl.BlockSpec(memory_space=pltpu.VMEM)
SCALARS = pl.BlockSpec(memory_space=pltpu.SMEM)

CHUNKS = (48, 32)


def barrier(*arrays):
    return lax.optimization_barrier(arrays)


def ranges(slots):
    starts = [sum(slots[:chunk]) for chunk in range(len(slots))]
    return [(start, count // 2) for start, count in zip(starts, slots)]


def iota(shape, dim):
    return lax.broadcasted_iota(jnp.int32, shape, dim)


def active(support, tile, axis):
    return jnp.max(jnp.where(support == tile, 1.0, 0.0), axis=axis, keepdims=True)


def project_kernel(first, chunks, where_ref, support_ref, traces_ref, movie_ref, *refs):
    outs, (held_ref, wide_ref, total_ref, gram_ref, arrived) = refs[:-5], refs[-5:]
    comps, frames = traces_ref.shape
    slots = sum(chunks)
    blocks = arrived.shape[0]
    depth = movie_ref.shape[0] // blocks
    rows = movie_ref.shape[0] // frames
    tiles = rows // TILE
    width = depth // rows

    def copy(block):
        part = pl.ds(block * depth, depth)
        return pltpu.make_async_copy(movie_ref.at[part, :], held_ref.at[part, :], arrived.at[block])

    for block in range(blocks):
        copy(block).start()
    spread = jnp.where(iota((width, depth), 0) == iota((width, depth), 1) // rows, 1.0, 0.0).astype(jnp.bfloat16)
    support = support_ref[...]
    upper = jnp.where(iota((comps, comps), 0) < iota((comps, comps), 1), 1.0, 0.0)
    slot = (iota((slots, comps), 0) + first).astype(jnp.float32)
    select = jnp.zeros((slots, comps), jnp.float32)
    before = jnp.zeros((1, 1), jnp.float32)
    base = jnp.full((slots, 1), -rows, jnp.int32)
    for order in range(tiles):
        tile = jnp.where(lax.rem(where_ref[0], 2) == 0, order, tiles - 1 - order)
        act = active(support, where_ref[0] * tiles + tile, 0)
        rank = jnp.dot(jnp.broadcast_to(act, (8, comps)), upper, preferred_element_type=jnp.float32)[0:1] + before
        select = select + jnp.where(slot == rank, act, 0.0)
        after = before + jnp.sum(act, axis=1, keepdims=True)
        here = (slot[:, 0:1] >= before) & (slot[:, 0:1] < after)
        base = jnp.where(here, TILE * tile, base)
        before = after
    select = select.astype(jnp.bfloat16)
    phase = iota((slots, depth), 1) % rows - base
    traces = traces_ref[...]
    chosen = jnp.dot(select, traces, preferred_element_type=jnp.float32).astype(jnp.bfloat16)
    for block in range(blocks):
        repeated = jnp.dot(
            chosen[:, block * width : (block + 1) * width], spread, preferred_element_type=jnp.float32
        )
        for row in range(TILE):
            wide_ref[row * slots : (row + 1) * slots, block * depth : (block + 1) * depth] = jnp.where(
                phase == row, repeated, 0.0
            ).astype(jnp.bfloat16)
    if first == 0:
        gram_ref[...] = lax.dot_general(
            traces, traces, (((1,), (1,)), ((), ())), preferred_element_type=jnp.float32
        )
    for block in range(blocks):
        copy(block).wait()
        part = jnp.dot(
            wide_ref[:, block * depth : (block + 1) * depth],
            held_ref[block * depth : (block + 1) * depth, :],
            preferred_element_type=jnp.float32,
        )
        if block == 0:
            total_ref[...] = part
        else:
            total_ref[...] += part
    odd = where_ref[1]
    for which in range(2):
        mine = odd if which == 0 else 1 - odd
        for chunk, (begin, half) in enumerate(ranges(chunks)):
            ref = outs[2 * chunk + which]
            for row in range(TILE):
                start = pl.multiple_of(row * slots + begin + mine * half, 8)
                ref[row * half : (row + 1) * half, :] = total_ref[pl.ds(start, half), :]
        if first == 0:
            ref = outs[which]
            filled = TILE * chunks[0] // 2
            band = ref.shape[0] - filled
            ref[filled:, :] = jnp.zeros((band, ref.shape[1]), jnp.float32)
            for piece in range(ref.shape[1] // LANES):
                start = pl.multiple_of((2 * piece + mine) * band, 8)
                ref[filled:, piece * LANES : piece * LANES + comps] = gram_ref[pl.ds(start, band), :]


def project(where, support, traces, recording, first, chunks):
    frames, rows, cols = recording.shape
    comps = traces.shape[0]
    slots = sum(chunks)
    shapes = []
    for chunk, (_, half) in enumerate(ranges(chunks)):
        band = comps * LANES // cols // 2 if first == 0 and chunk == 0 else 0
        shapes += [(TILE * half + band, cols)] * 2
    return pl.pallas_call(
        functools.partial(project_kernel, first, chunks),
        name="project",
        in_specs=[SCALARS, WHOLE, WHOLE, pl.BlockSpec(memory_space=pltpu.HBM)],
        out_specs=[WHOLE] * len(shapes),
        out_shape=[jax.ShapeDtypeStruct(shape, jnp.float32) for shape in shapes],
        scratch_shapes=[
            VMEM((frames * rows, cols), jnp.bfloat16),
            VMEM((TILE * slots, frames * rows), jnp.bfloat16),
            VMEM((TILE * slots, cols), jnp.float32),
            VMEM((comps, comps), jnp.float32),
            pltpu.SemaphoreType.DMA((frames // FRAME_BLOCK,)),
        ],
        compiler_params=pltpu.CompilerParams(vmem_limit_bytes=16 << 20),
    )(where, support, traces, recording.reshape(frames * rows, cols))


def tiles_of(array):
    comps, rows, cols = array.shape
    pieces = array.reshape(comps, rows, cols // LANES, LANES).transpose(0, 2, 1, 3)
    return pieces.reshape(comps * rows * cols // LANES, LANES)


def from_tiles(tiles, comps, rows, cols):
    pieces = tiles.reshape(comps, cols // LANES, rows, LANES).transpose(0, 2, 1, 3)
    return pieces.reshape(comps, rows, cols)


def plane_of(tiles_ref, row, comps, rows, cols):
    step = rows * cols // LANES
    pieces = [tiles_ref[pl.ds(piece * rows + row, comps, stride=step), :] for piece in range(cols // LANES)]
    return jnp.concatenate(pieces, axis=1)


def terms_of(packed):
    terms = []
    for _ in range(TERMS):
        term = packed.astype(jnp.bfloat16)
        packed = packed - term.astype(jnp.float32)
        terms.append(term)
    return jnp.concatenate(terms, axis=0)


def slots_of(ref, half, row):
    height = ref.shape[0] // 2
    return [ref[part * height + row * half : part * height + (row + 1) * half, :] for part in range(2)]


def moved(pick, parts):
    terms = terms_of(jnp.concatenate(parts, axis=0))
    return jnp.dot(pick[:, 0 : terms.shape[0]], terms, preferred_element_type=jnp.float32)


def prepare_kernel(
    count,
    where_ref,
    support_ref,
    sums_ref,
    tiles_ref,
    correlation_ref,
    base_ref,
    pick_ref,
    spare_ref,
    rate_ref,
    outer_ref,
    more_ref,
):
    rows, comps, cols = base_ref.shape
    tiles = rows // TILE
    index = where_ref[0]
    odd = lax.rem(index, 2)
    main = sum(CHUNKS)
    band = comps * LANES // cols // 2
    height = sums_ref.shape[0] // 2
    gram = jnp.concatenate(
        [
            sums_ref[(half + 1) * height - band : (half + 1) * height, piece * LANES : piece * LANES + comps]
            for piece in range(cols // LANES)
            for half in range(2)
        ],
        axis=0,
    )
    own = iota(gram.shape, 0) == iota(gram.shape, 1)
    diagonal = jnp.sum(jnp.where(own, gram, 0.0), axis=1, keepdims=True)
    rate = step_scale / (diagonal + epsilon)
    rate_ref[...] = jnp.broadcast_to(rate, rate_ref.shape)
    support = support_ref[...]
    lower = jnp.where(iota((comps, comps), 1) < iota((comps, comps), 0), 1.0, 0.0)
    place = iota((comps, pick_ref.shape[1]), 1)
    spare = comps * tiles - main

    def terms(count, first):
        return jnp.where(place < TERMS * count, first + place % count, -1).astype(jnp.float32)

    before = jnp.zeros((1, 1), jnp.float32)
    for order in range(tiles):
        tile = jnp.where(odd == 0, order, tiles - 1 - order)
        act = active(support, index * tiles + tile, 1)
        rank = before + jnp.dot(
            lower, jnp.broadcast_to(act, (comps, LANES)), preferred_element_type=jnp.float32
        )[:, 0:1]
        chosen = pl.ds(pl.multiple_of(tile * comps, comps), comps)
        pick_ref[chosen, :] = jnp.where(terms(main, 0) == rank, act, 0.0).astype(jnp.bfloat16)
        spare_ref[chosen, :] = jnp.where(terms(spare, main) == rank, act, 0.0).astype(jnp.bfloat16)
        if order == 0:
            first_pick = jnp.where(terms(CHUNKS[0], 0) == rank, act, 0.0).astype(jnp.bfloat16)
        before = before + jnp.sum(act, axis=0, keepdims=True)
    for row in range(rows):
        act = active(support, index * tiles + row // TILE, 1)
        field = plane_of(tiles_ref, row, comps, rows, cols)
        slope = jnp.dot(gram, field, precision=HIGHEST, preferred_element_type=jnp.float32)
        base_ref[row] = jnp.where(act > 0.0, field - rate * slope, 0.0)
    for row in range(TILE):
        base = jnp.where(odd == 0, base_ref[row], base_ref[rows - TILE + row])
        sums = moved(first_pick, slots_of(sums_ref, CHUNKS[0] // 2, row))
        outer_ref[row * comps : (row + 1) * comps, :] = jnp.maximum(base + rate * sums, 0.0)
    outer_ref[TILE * comps :, :] = correlation_ref[...]
    over = jnp.full((1, 1), -1.0, jnp.float32)
    for device in range(count):
        held = jnp.zeros((1, 1), jnp.float32)
        for tile in range(tiles):
            in_tile = jnp.sum(active(support, device * tiles + tile, 1), axis=0, keepdims=True)
            over = jnp.maximum(over, in_tile - CHUNKS[0])
            held = held + in_tile
        over = jnp.maximum(over, held - main)
    more_ref[0] = (jnp.max(over) > 0.5).astype(jnp.int32)


def prepare(where, support, sums, tiles_in, correlation, count):
    rows = correlation.shape[0]
    comps, cols = support.shape[0], sums.shape[1]
    tiles = rows // TILE
    picks = jax.ShapeDtypeStruct((tiles * comps, 4 * comps), jnp.bfloat16)
    return pl.pallas_call(
        functools.partial(prepare_kernel, count),
        name="prepare",
        in_specs=[SCALARS] + [WHOLE] * 4,
        out_specs=[WHOLE] * 5 + [SCALARS],
        out_shape=[
            jax.ShapeDtypeStruct((rows, comps, cols), jnp.float32),
            picks,
            picks,
            jax.ShapeDtypeStruct((comps, LANES), jnp.float32),
            jax.ShapeDtypeStruct((TILE * comps + rows, cols), jnp.float32),
            jax.ShapeDtypeStruct((1,), jnp.int32),
        ],
        compiler_params=pltpu.CompilerParams(vmem_limit_bytes=12 << 20),
    )(where, support, sums, tiles_in, correlation)


def step_kernel(with_spare, where_ref, base_ref, pick_ref, spare_ref, rate_ref, correlation_ref, *refs):
    refs, outs = refs[: len(CHUNKS) + with_spare], refs[len(CHUNKS) + with_spare :]
    rows, comps, cols = base_ref.shape
    tiles = rows // TILE
    rate = rate_ref[:, 0:1]
    even = lax.rem(where_ref[0], 2) == 0
    for row in range(TILE):
        parts = []
        for ref, (_, half) in zip(refs, ranges(CHUNKS)):
            parts += slots_of(ref, half, row)
        sums = moved(pick_ref, parts)
        if with_spare:
            sums = sums + moved(spare_ref, slots_of(refs[-1], refs[-1].shape[0] // 2 // TILE, row))
        planes = []
        for tile in range(tiles):
            at = tile * TILE + row
            planes.append(jnp.maximum(base_ref[at] + rate * sums[tile * comps : (tile + 1) * comps, :], 0.0))
            outs[0][at] = planes[-1]
        chosen = slice(row * comps, (row + 1) * comps)
        outs[1][chosen, :] = jnp.where(even, planes[-1], planes[0])
        if with_spare:
            outs[2][chosen, :] = jnp.where(even, planes[0], planes[-1])
    for ref in outs[1:]:
        ref[TILE * comps :, :] = correlation_ref[...]


def step_rows(where, prepared, correlation, sums):
    base = prepared[0]
    rows, comps, cols = base.shape
    spare = len(sums) - len(CHUNKS)
    edge = jax.ShapeDtypeStruct((TILE * comps + rows, cols), jnp.float32)
    return pl.pallas_call(
        functools.partial(step_kernel, spare),
        name="step_rows",
        in_specs=[SCALARS] + [WHOLE] * (5 + len(sums)),
        out_specs=[WHOLE] * (2 + spare),
        out_shape=[jax.ShapeDtypeStruct(base.shape, jnp.float32), edge] + [edge] * spare,
        compiler_params=pltpu.CompilerParams(vmem_limit_bytes=12 << 20),
    )(where, *prepared, correlation, *sums)


def diffuse_kernel(
    where_ref,
    support_ref,
    correlation_ref,
    field_ref,
    inner_ref,
    outer_ref,
    out_ref,
    done_ref,
    edge_ref,
    weight_ref,
    keep_ref,
    mask_ref,
    sent,
):
    rows, comps, cols = field_ref.shape
    tiles = rows // TILE
    pieces = cols // LANES
    group = GROUP
    index, last = where_ref[0], where_ref[2]
    odd = lax.rem(index, 2) == 1
    has_above = jnp.where(index > 0, 1.0, 0.0)
    has_below = jnp.where(index < last, 1.0, 0.0)
    for row in range(PASSES):
        chosen = slice(row * comps, (row + 1) * comps)
        inner, outer = inner_ref[chosen, :], outer_ref[chosen, :]
        edge_ref[row] = has_above * jnp.where(odd, inner, outer)
        edge_ref[PASSES + row] = has_below * jnp.where(odd, outer, inner)
    inner, outer = inner_ref[PASSES * comps :, :], outer_ref[PASSES * comps :, :]
    parts = (
        (0, (diffusion_rate * has_above) * jnp.where(odd, inner, outer)[rows - PASSES :]),
        (PASSES, diffusion_rate * correlation_ref[...]),
        (PASSES + rows, (diffusion_rate * has_below) * jnp.where(odd, outer, inner)[:PASSES]),
    )
    for first, weight in parts:
        for row in range(weight.shape[0]):
            line = jnp.broadcast_to(weight[row : row + 1, :], (GROUP, cols))
            weight_ref[first + row] = line
            keep_ref[first + row] = 1.0 - 4.0 * line
    support = support_ref[...]
    for tile in range(tiles):
        act = active(support, index * tiles + tile, 1)
        mask_ref[tile] = jnp.broadcast_to(act, mask_ref.shape[1:])
    lane = iota((group, LANES), 1)
    at_left, at_right = lane == 0, lane == LANES - 1
    nothing = jnp.zeros((group, LANES), jnp.float32)
    total = rows + 2 * PASSES
    size = group * rows * pieces

    def copy(step):
        part = pl.ds(step * size, size)
        return pltpu.make_async_copy(done_ref.at[part, :], out_ref.at[part, :], sent.at[step])

    def relax(step, carry):
        start = pl.multiple_of(step * group, group)
        planes = [{} for _ in range(PASSES + 1)]

        def load(row):
            if row < PASSES:
                ref, at = edge_ref, row
            elif row < PASSES + rows:
                ref, at = field_ref, row - PASSES
            else:
                ref, at = edge_ref, row - rows
            return [ref[at, pl.ds(start, group), piece * LANES : (piece + 1) * LANES] for piece in range(pieces)]

        def renew(done, row):
            above, center, below = (planes[done][row + shift] for shift in (-1, 0, 1))
            to_right = [pltpu.roll(piece, 1, 1) for piece in center]
            to_left = [pltpu.roll(piece, LANES - 1, 1) for piece in center]
            fresh = []
            for piece in range(pieces):
                left = jnp.where(at_left, to_right[piece - 1] if piece > 0 else nothing, to_right[piece])
                right = jnp.where(at_right, to_left[piece + 1] if piece < pieces - 1 else nothing, to_left[piece])
                beside = (above[piece] + below[piece]) + (left + right)
                lanes = slice(piece * LANES, (piece + 1) * LANES)
                fresh.append(keep_ref[row, :, lanes] * center[piece] + weight_ref[row, :, lanes] * beside)
            return fresh

        masks = [mask_ref[tile, pl.ds(start, group), :] for tile in range(tiles)]
        for front in range(total + PASSES):
            if front < total:
                planes[0][front] = load(front)
            for done in range(PASSES):
                row = front - 1 - done
                if done < row < total - 1 - done:
                    planes[done + 1][row] = renew(done, row)
                    planes[done].pop(row - 1)
                    if done == PASSES - 1:
                        own = row - PASSES
                        for piece in range(pieces):
                            at = pl.ds(step * size + piece * rows + own, group, stride=rows * pieces)
                            done_ref[at, :] = planes[PASSES][row][piece] * masks[own // TILE]
        copy(step).start()
        return carry

    lax.fori_loop(0, comps // group, relax, 0)
    for step in range(comps // group):
        copy(step).wait()


def diffuse(where, support, correlation, field, inner, outer):
    rows, comps, cols = field.shape
    pieces = cols // LANES
    lines = VMEM((rows + 2 * PASSES, GROUP, cols), jnp.float32)
    shape = (comps * rows * pieces, LANES)
    return pl.pallas_call(
        diffuse_kernel,
        name="diffuse",
        in_specs=[SCALARS] + [WHOLE] * 5,
        out_specs=pl.BlockSpec(memory_space=pltpu.HBM),
        out_shape=jax.ShapeDtypeStruct(shape, jnp.float32),
        scratch_shapes=[
            VMEM(shape, jnp.float32),
            VMEM((2 * PASSES, comps, cols), jnp.float32),
            lines,
            lines,
            VMEM((rows // TILE, comps, LANES), jnp.float32),
            pltpu.SemaphoreType.DMA((comps // GROUP,)),
        ],
        compiler_params=pltpu.CompilerParams(vmem_limit_bytes=16 << 20),
    )(where, support, correlation, field, inner, outer)


def pairs_of(count, first):
    table = list(range(count))
    for i in range(first, count - 1, 2):
        table[i], table[i + 1] = i + 1, i
    return list(enumerate(table))


NEAR, FAR = pairs_of(4, 0), [(0, 3), (1, 2), (2, 1), (3, 0)]


def in_order(odd, mine, other):
    return jnp.concatenate([jnp.where(odd, other, mine), jnp.where(odd, mine, other)], axis=0)


def per_device(recording, traces, footprints, correlation, support):
    comps, rows, cols = footprints.shape
    tiles = rows // TILE
    index = lax.axis_index("rows")
    count = lax.axis_size("rows")
    part = lax.axis_index("tm")
    line = lax.axis_size("tm") == 4
    odd = ((part == 1) | (part == 2)) & line
    where = jnp.stack([index, odd.astype(jnp.int32), jnp.int32(count - 1)]).astype(jnp.int32)
    inside, outside = pairs_of(count, 0), pairs_of(count, 1)
    names = support.T
    field_tiles = tiles_of(footprints)
    spare = comps * tiles - sum(CHUNKS)

    def near(array):
        return lax.ppermute(array, "tm", NEAR)

    def far(array):
        return lax.ppermute(array, "tm", FAR)

    def beside(array):
        return lax.ppermute(array, "rows", outside)

    mine, other = [None, None], [None, None]
    mine[0], other[0] = project(where, names, traces, recording, 0, CHUNKS[:1])
    *_, later = barrier(other[0], traces)
    mine[1], other[1] = project(where, names, later, recording, CHUNKS[0], CHUNKS[1:])
    if line:
        first_received = near(other[0])
        half = [barrier(mine[0] + first_received)[0]]
        later, half[0] = barrier(other[1], half[0])
        first_across = far(half[0])
        half.append(barrier(mine[1] + near(later))[0])
        whole = [barrier(half[0] + first_across)[0]]
        half[1], whole[0] = barrier(half[1], whole[0])
        first_back = near(whole[0])
        whole.append(barrier(half[1] + far(half[1]))[0])
        back = [first_back, near(whole[1])]
    else:
        whole, back = lax.psum((mine, other), "tm")
    sums = [barrier(in_order(odd, *barrier(whole[0], back[0])))[0]]
    *prepared, to_outer, more = prepare(where, support, sums[0], field_tiles, correlation, count)
    outer = beside(to_outer)
    own, theirs, *prepared = barrier(whole[1], back[1], *prepared)
    sums.append(barrier(in_order(odd, own, theirs))[0])

    def rest():
        mine, other = project(where, names, traces, recording, sum(CHUNKS), (spare,))
        if line:
            half = mine + near(other)
            mine = half + far(half)
            other = near(mine)
        else:
            mine, other = lax.psum((mine, other), "tm")
        field, to_inner, to_outer = step_rows(where, prepared, correlation, sums + [in_order(odd, mine, other)])
        return field, to_inner, beside(to_outer)

    def enough():
        field, to_inner = step_rows(where, prepared, correlation, sums)
        return field, to_inner, outer

    field, to_inner, outer = lax.cond(more[0] > 0, rest, enough)
    inner = lax.ppermute(to_inner, "rows", inside)
    result = diffuse(where, support, correlation, field, inner, outer)
    return from_tiles(result, comps, rows, cols)


def solution(mesh):
    return jax.shard_map(
        per_device,
        mesh=mesh,
        in_specs=(
            P("tm", ("band", "rows"), None),
            P("band", "tm"),
            P(None, ("band", "rows"), None),
            P(("band", "rows"), None),
            P("band", None),
        ),
        out_specs=P(None, ("band", "rows"), None),
        check_vma=False,
    )
```

```python
import functools

import jax
import jax.numpy as jnp
from jax import lax
from jax.sharding import PartitionSpec as P
from jax.experimental import pallas as pl
from jax.experimental.pallas import tpu as pltpu

TILE = 4
PASSES = 4
diffusion_rate = 0.24
step_scale = 0.5
epsilon = 1e-06
FRAME_BLOCK = 128
LANES = 128
GROUP = 8
TERMS = 3
HIGHEST = lax.Precision.HIGHEST
VMEM = pltpu.VMEM
WHOLE = pl.BlockSpec(memory_space=pltpu.VMEM)
SCALARS = pl.BlockSpec(memory_space=pltpu.SMEM)

CHUNKS = (48, 32)


def barrier(*arrays):
    return lax.optimization_barrier(arrays)


def ranges(slots):
    starts = [sum(slots[:chunk]) for chunk in range(len(slots))]
    return [(start, count // 2) for start, count in zip(starts, slots)]


def iota(shape, dim):
    return lax.broadcasted_iota(jnp.int32, shape, dim)


def active(support, tile, axis):
    return jnp.max(jnp.where(support == tile, 1.0, 0.0), axis=axis, keepdims=True)


def project_kernel(first, chunks, where_ref, support_ref, traces_ref, movie_ref, *refs):
    outs, (held_ref, wide_ref, total_ref, gram_ref, arrived) = refs[:-5], refs[-5:]
    comps, frames = traces_ref.shape
    slots = sum(chunks)
    blocks = arrived.shape[0]
    depth = movie_ref.shape[0] // blocks
    rows = movie_ref.shape[0] // frames
    tiles = rows // TILE
    width = depth // rows

    def copy(block):
        part = pl.ds(block * depth, depth)
        return pltpu.make_async_copy(movie_ref.at[part, :], held_ref.at[part, :], arrived.at[block])

    for block in range(blocks):
        copy(block).start()
    spread = jnp.where(iota((width, depth), 0) == iota((width, depth), 1) // rows, 1.0, 0.0).astype(jnp.bfloat16)
    support = support_ref[...]
    upper = jnp.where(iota((comps, comps), 0) < iota((comps, comps), 1), 1.0, 0.0)
    slot = (iota((slots, comps), 0) + first).astype(jnp.float32)
    select = jnp.zeros((slots, comps), jnp.float32)
    before = jnp.zeros((1, 1), jnp.float32)
    base = jnp.full((slots, 1), -rows, jnp.int32)
    for order in range(tiles):
        tile = jnp.where(lax.rem(where_ref[0], 2) == 0, order, tiles - 1 - order)
        act = active(support, where_ref[0] * tiles + tile, 0)
        rank = jnp.dot(jnp.broadcast_to(act, (8, comps)), upper, preferred_element_type=jnp.float32)[0:1] + before
        select = select + jnp.where(slot == rank, act, 0.0)
        after = before + jnp.sum(act, axis=1, keepdims=True)
        here = (slot[:, 0:1] >= before) & (slot[:, 0:1] < after)
        base = jnp.where(here, TILE * tile, base)
        before = after
    select = select.astype(jnp.bfloat16)
    phase = iota((slots, depth), 1) % rows - base
    traces = traces_ref[...]
    chosen = jnp.dot(select, traces, preferred_element_type=jnp.float32).astype(jnp.bfloat16)
    for block in range(blocks):
        repeated = jnp.dot(
            chosen[:, block * width : (block + 1) * width], spread, preferred_element_type=jnp.float32
        )
        for row in range(TILE):
            wide_ref[row * slots : (row + 1) * slots, block * depth : (block + 1) * depth] = jnp.where(
                phase == row, repeated, 0.0
            ).astype(jnp.bfloat16)
    if first == 0:
        gram_ref[...] = lax.dot_general(
            traces, traces, (((1,), (1,)), ((), ())), preferred_element_type=jnp.float32
        )
    for block in range(blocks):
        copy(block).wait()
        part = jnp.dot(
            wide_ref[:, block * depth : (block + 1) * depth],
            held_ref[block * depth : (block + 1) * depth, :],
            preferred_element_type=jnp.float32,
        )
        if block == 0:
            total_ref[...] = part
        else:
            total_ref[...] += part
    odd = where_ref[1]
    for which in range(2):
        mine = odd if which == 0 else 1 - odd
        for chunk, (begin, half) in enumerate(ranges(chunks)):
            ref = outs[2 * chunk + which]
            for row in range(TILE):
                start = pl.multiple_of(row * slots + begin + mine * half, 8)
                ref[row * half : (row + 1) * half, :] = total_ref[pl.ds(start, half), :]
        if first == 0:
            ref = outs[which]
            filled = TILE * chunks[0] // 2
            band = ref.shape[0] - filled
            ref[filled:, :] = jnp.zeros((band, ref.shape[1]), jnp.float32)
            for piece in range(ref.shape[1] // LANES):
                start = pl.multiple_of((2 * piece + mine) * band, 8)
                ref[filled:, piece * LANES : piece * LANES + comps] = gram_ref[pl.ds(start, band), :]


def project(where, support, traces, recording, first, chunks):
    frames, rows, cols = recording.shape
    comps = traces.shape[0]
    slots = sum(chunks)
    shapes = []
    for chunk, (_, half) in enumerate(ranges(chunks)):
        band = comps * LANES // cols // 2 if first == 0 and chunk == 0 else 0
        shapes += [(TILE * half + band, cols)] * 2
    return pl.pallas_call(
        functools.partial(project_kernel, first, chunks),
        name="project",
        in_specs=[SCALARS, WHOLE, WHOLE, pl.BlockSpec(memory_space=pltpu.HBM)],
        out_specs=[WHOLE] * len(shapes),
        out_shape=[jax.ShapeDtypeStruct(shape, jnp.float32) for shape in shapes],
        scratch_shapes=[
            VMEM((frames * rows, cols), jnp.bfloat16),
            VMEM((TILE * slots, frames * rows), jnp.bfloat16),
            VMEM((TILE * slots, cols), jnp.float32),
            VMEM((comps, comps), jnp.float32),
            pltpu.SemaphoreType.DMA((frames // FRAME_BLOCK,)),
        ],
        compiler_params=pltpu.CompilerParams(vmem_limit_bytes=13 << 20),
    )(where, support, traces, recording.reshape(frames * rows, cols))


def tiles_of(array):
    comps, rows, cols = array.shape
    pieces = array.reshape(comps, rows, cols // LANES, LANES).transpose(0, 2, 1, 3)
    return pieces.reshape(comps * rows * cols // LANES, LANES)


def from_tiles(tiles, comps, rows, cols):
    pieces = tiles.reshape(comps, cols // LANES, rows, LANES).transpose(0, 2, 1, 3)
    return pieces.reshape(comps, rows, cols)


def plane_of(tiles_ref, row, comps, rows, cols):
    step = rows * cols // LANES
    pieces = [tiles_ref[pl.ds(piece * rows + row, comps, stride=step), :] for piece in range(cols // LANES)]
    return jnp.concatenate(pieces, axis=1)


def terms_of(packed):
    terms = []
    for _ in range(TERMS):
        term = packed.astype(jnp.bfloat16)
        packed = packed - term.astype(jnp.float32)
        terms.append(term)
    return jnp.concatenate(terms, axis=0)


def slots_of(ref, half, row):
    height = ref.shape[0] // 2
    return [ref[part * height + row * half : part * height + (row + 1) * half, :] for part in range(2)]


def moved(pick, parts):
    terms = terms_of(jnp.concatenate(parts, axis=0))
    return jnp.dot(pick[:, 0 : terms.shape[0]], terms, preferred_element_type=jnp.float32)


def gram_of(sums_ref, comps):
    cols = sums_ref.shape[1]
    band = comps * LANES // cols // 2
    height = sums_ref.shape[0] // 2
    gram = jnp.concatenate(
        [
            sums_ref[(half + 1) * height - band : (half + 1) * height, piece * LANES : piece * LANES + comps]
            for piece in range(cols // LANES)
            for half in range(2)
        ],
        axis=0,
    )
    own = iota(gram.shape, 0) == iota(gram.shape, 1)
    diagonal = jnp.sum(jnp.where(own, gram, 0.0), axis=1, keepdims=True)
    return gram, step_scale / (diagonal + epsilon)


def descend(gram, rate, field, act):
    slope = jnp.dot(gram, field, precision=HIGHEST, preferred_element_type=jnp.float32)
    return jnp.where(act > 0.0, field - rate * slope, 0.0)


def rank_of(act):
    comps = act.shape[0]
    lower = jnp.where(iota((comps, comps), 1) < iota((comps, comps), 0), 1.0, 0.0)
    return jnp.dot(lower, jnp.broadcast_to(act, (comps, LANES)), preferred_element_type=jnp.float32)[:, 0:1]


def term_slots(comps, count, first):
    place = iota((comps, 4 * comps), 1)
    return jnp.where(place < TERMS * count, first + place % count, -1).astype(jnp.float32)


def plan_kernel(
    count, where_ref, support_ref, tiles_ref, planes_ref, act_ref, first_ref, pick_ref, spare_ref, more_ref
):
    rows, comps, cols = planes_ref.shape
    tiles = rows // TILE
    index = where_ref[0]
    main = sum(CHUNKS)
    spare = comps * tiles - main
    support = support_ref[...]
    for row in range(rows):
        planes_ref[row] = plane_of(tiles_ref, row, comps, rows, cols)
    before = jnp.zeros((1, 1), jnp.float32)
    for order in range(tiles):
        tile = jnp.where(lax.rem(index, 2) == 0, order, tiles - 1 - order)
        act = active(support, index * tiles + tile, 1)
        act_ref[tile] = jnp.broadcast_to(act, (comps, LANES))
        rank = before + rank_of(act)
        chosen = pl.ds(pl.multiple_of(tile * comps, comps), comps)
        pick_ref[chosen, :] = jnp.where(term_slots(comps, main, 0) == rank, act, 0.0).astype(jnp.bfloat16)
        spare_ref[chosen, :] = jnp.where(term_slots(comps, spare, main) == rank, act, 0.0).astype(jnp.bfloat16)
        if order == 0:
            first = jnp.where(term_slots(comps, CHUNKS[0], 0) == rank, act, 0.0)
            first_ref[...] = first.astype(jnp.bfloat16)
        before = before + jnp.sum(act, axis=0, keepdims=True)
    over = jnp.full((1, 1), -1.0, jnp.float32)
    for device in range(count):
        held = jnp.zeros((1, 1), jnp.float32)
        for tile in range(tiles):
            in_tile = jnp.sum(active(support, device * tiles + tile, 1), axis=0, keepdims=True)
            over = jnp.maximum(over, in_tile - CHUNKS[0])
            held = held + in_tile
        over = jnp.maximum(over, held - main)
    more_ref[0] = (jnp.max(over) > 0.5).astype(jnp.int32)


def plan(where, support, tiles_in, rows, count):
    comps = support.shape[0]
    cols = tiles_in.shape[0] * LANES // (rows * comps)
    tiles = rows // TILE

    def picks(number):
        return jax.ShapeDtypeStruct((number * comps, 4 * comps), jnp.bfloat16)

    return pl.pallas_call(
        functools.partial(plan_kernel, count),
        name="plan",
        in_specs=[SCALARS] + [WHOLE] * 2,
        out_specs=[WHOLE] * 5 + [SCALARS],
        out_shape=[
            jax.ShapeDtypeStruct((rows, comps, cols), jnp.float32),
            jax.ShapeDtypeStruct((tiles, comps, LANES), jnp.float32),
            picks(1),
            picks(tiles),
            picks(tiles),
            jax.ShapeDtypeStruct((1,), jnp.int32),
        ],
        compiler_params=pltpu.CompilerParams(vmem_limit_bytes=6 << 20),
    )(where, support, tiles_in)


def edge_kernel(where_ref, sums_ref, planes_ref, act_ref, first_ref, correlation_ref, outer_ref):
    rows, comps, cols = planes_ref.shape
    odd = lax.rem(where_ref[0], 2)
    gram, rate = gram_of(sums_ref, comps)
    act = act_ref[odd * (rows // TILE - 1)][:, 0:1]
    for row in range(TILE):
        field = planes_ref[odd * (rows - TILE) + row]
        sums = moved(first_ref, slots_of(sums_ref, CHUNKS[0] // 2, row))
        field = jnp.maximum(descend(gram, rate, field, act) + rate * sums, 0.0)
        outer_ref[row * comps : (row + 1) * comps, :] = field
    outer_ref[TILE * comps :, :] = correlation_ref[...]


def edge_rows(where, sums, planes, act, first, correlation):
    rows, comps, cols = planes.shape
    return pl.pallas_call(
        edge_kernel,
        name="edge_rows",
        in_specs=[SCALARS] + [WHOLE] * 5,
        out_specs=WHOLE,
        out_shape=jax.ShapeDtypeStruct((TILE * comps + rows, cols), jnp.float32),
        compiler_params=pltpu.CompilerParams(vmem_limit_bytes=6 << 20),
    )(where, sums, planes, act, first, correlation)


def prepare_kernel(sums_ref, planes_ref, act_ref, base_ref, rate_ref):
    rows, comps, cols = base_ref.shape
    gram, rate = gram_of(sums_ref, comps)
    rate_ref[...] = jnp.broadcast_to(rate, rate_ref.shape)
    for row in range(rows):
        base_ref[row] = descend(gram, rate, planes_ref[row], act_ref[row // TILE][:, 0:1])


def prepare(sums, planes, act):
    return pl.pallas_call(
        prepare_kernel,
        name="prepare",
        in_specs=[WHOLE] * 3,
        out_specs=[WHOLE] * 2,
        out_shape=[
            jax.ShapeDtypeStruct(planes.shape, jnp.float32),
            jax.ShapeDtypeStruct((planes.shape[1], LANES), jnp.float32),
        ],
        compiler_params=pltpu.CompilerParams(vmem_limit_bytes=6 << 20),
    )(sums, planes, act)


def step_kernel(with_spare, where_ref, base_ref, pick_ref, spare_ref, rate_ref, correlation_ref, *refs):
    refs, outs = refs[: len(CHUNKS) + with_spare], refs[len(CHUNKS) + with_spare :]
    rows, comps, cols = base_ref.shape
    tiles = rows // TILE
    rate = rate_ref[:, 0:1]
    even = lax.rem(where_ref[0], 2) == 0
    for row in range(TILE):
        parts = []
        for ref, (_, half) in zip(refs, ranges(CHUNKS)):
            parts += slots_of(ref, half, row)
        sums = moved(pick_ref, parts)
        if with_spare:
            sums = sums + moved(spare_ref, slots_of(refs[-1], refs[-1].shape[0] // 2 // TILE, row))
        planes = []
        for tile in range(tiles):
            at = tile * TILE + row
            planes.append(jnp.maximum(base_ref[at] + rate * sums[tile * comps : (tile + 1) * comps, :], 0.0))
            outs[0][at] = planes[-1]
        chosen = slice(row * comps, (row + 1) * comps)
        outs[1][chosen, :] = jnp.where(even, planes[-1], planes[0])
        outs[2][chosen, :] = jnp.where(even, planes[0], planes[-1])
    for ref in outs[1:]:
        ref[TILE * comps :, :] = correlation_ref[...]


def step_rows(where, prepared, correlation, sums):
    base = prepared[0]
    rows, comps, cols = base.shape
    spare = len(sums) - len(CHUNKS)
    edge = jax.ShapeDtypeStruct((TILE * comps + rows, cols), jnp.float32)
    return pl.pallas_call(
        functools.partial(step_kernel, spare),
        name="step_rows",
        in_specs=[SCALARS] + [WHOLE] * (5 + len(sums)),
        out_specs=[WHOLE] * 3,
        out_shape=[jax.ShapeDtypeStruct(base.shape, jnp.float32), edge, edge],
        compiler_params=pltpu.CompilerParams(vmem_limit_bytes=6 << 20),
    )(where, *prepared, correlation, *sums)


def diffuse_kernel(
    where_ref,
    more_ref,
    act_ref,
    correlation_ref,
    field_ref,
    inner_ref,
    outer_ref,
    again_ref,
    out_ref,
    done_ref,
    edge_ref,
    weight_ref,
    keep_ref,
    sent,
):
    rows, comps, cols = field_ref.shape
    tiles = rows // TILE
    pieces = cols // LANES
    group = GROUP
    index, last = where_ref[0], where_ref[2]
    odd = lax.rem(index, 2) == 1
    again = more_ref[0] > 0
    has_above = jnp.where(index > 0, 1.0, 0.0)
    has_below = jnp.where(index < last, 1.0, 0.0)
    for row in range(PASSES):
        chosen = slice(row * comps, (row + 1) * comps)
        inner = inner_ref[chosen, :]
        outer = jnp.where(again, again_ref[chosen, :], outer_ref[chosen, :])
        edge_ref[row] = has_above * jnp.where(odd, inner, outer)
        edge_ref[PASSES + row] = has_below * jnp.where(odd, outer, inner)
    inner, outer = inner_ref[PASSES * comps :, :], outer_ref[PASSES * comps :, :]
    parts = (
        (0, (diffusion_rate * has_above) * jnp.where(odd, inner, outer)[rows - PASSES :]),
        (PASSES, diffusion_rate * correlation_ref[...]),
        (PASSES + rows, (diffusion_rate * has_below) * jnp.where(odd, outer, inner)[:PASSES]),
    )
    for first, weight in parts:
        for row in range(weight.shape[0]):
            line = jnp.broadcast_to(weight[row : row + 1, :], (GROUP, cols))
            weight_ref[first + row] = line
            keep_ref[first + row] = 1.0 - 4.0 * line
    lane = iota((group, LANES), 1)
    at_left, at_right = lane == 0, lane == LANES - 1
    nothing = jnp.zeros((group, LANES), jnp.float32)
    total = rows + 2 * PASSES
    size = group * rows * pieces

    def copy(step):
        part = pl.ds(step * size, size)
        return pltpu.make_async_copy(done_ref.at[part, :], out_ref.at[part, :], sent.at[step])

    def relax(step, carry):
        start = pl.multiple_of(step * group, group)

        def load(row):
            if row < PASSES:
                ref, at = edge_ref, row
            elif row < PASSES + rows:
                ref, at = field_ref, row - PASSES
            else:
                ref, at = edge_ref, row - rows
            return [ref[at, pl.ds(start, group), piece * LANES : (piece + 1) * LANES] for piece in range(pieces)]

        def renew(planes, done, at):
            above, center, below = planes[at - 1 : at + 2]
            row = at + done
            to_right = [pltpu.roll(piece, 1, 1) for piece in center]
            to_left = [pltpu.roll(piece, LANES - 1, 1) for piece in center]
            fresh = []
            for piece in range(pieces):
                left = jnp.where(at_left, to_right[piece - 1] if piece > 0 else nothing, to_right[piece])
                right = jnp.where(at_right, to_left[piece + 1] if piece < pieces - 1 else nothing, to_left[piece])
                beside = (above[piece] + below[piece]) + (left + right)
                lanes = slice(piece * LANES, (piece + 1) * LANES)
                fresh.append(keep_ref[row, :, lanes] * center[piece] + weight_ref[row, :, lanes] * beside)
            return fresh

        masks = [act_ref[tile, pl.ds(start, group), :] for tile in range(tiles)]
        planes = [load(row) for row in range(total)]
        for done in range(PASSES):
            planes = [renew(planes, done, at) for at in range(1, len(planes) - 1)]
        for own in range(rows):
            for piece in range(pieces):
                at = pl.ds(step * size + piece * rows + own, group, stride=rows * pieces)
                done_ref[at, :] = planes[own][piece] * masks[own // TILE]
        copy(step).start()
        return carry

    lax.fori_loop(0, comps // group, relax, 0)
    for step in range(comps // group):
        copy(step).wait()


def diffuse(where, more, act, correlation, field, inner, outer, outer_again):
    rows, comps, cols = field.shape
    pieces = cols // LANES
    lines = VMEM((rows + 2 * PASSES, GROUP, cols), jnp.float32)
    shape = (comps * rows * pieces, LANES)
    return pl.pallas_call(
        diffuse_kernel,
        name="diffuse",
        in_specs=[SCALARS] * 2 + [WHOLE] * 6,
        out_specs=pl.BlockSpec(memory_space=pltpu.HBM),
        out_shape=jax.ShapeDtypeStruct(shape, jnp.float32),
        scratch_shapes=[
            VMEM(shape, jnp.float32),
            VMEM((2 * PASSES, comps, cols), jnp.float32),
            lines,
            lines,
            pltpu.SemaphoreType.DMA((comps // GROUP,)),
        ],
        compiler_params=pltpu.CompilerParams(vmem_limit_bytes=8 << 20),
    )(where, more, act, correlation, field, inner, outer, outer_again)


def pairs_of(count, first):
    table = list(range(count))
    for i in range(first, count - 1, 2):
        table[i], table[i + 1] = i + 1, i
    return list(enumerate(table))


NEAR, FAR = pairs_of(4, 0), [(0, 3), (1, 2), (2, 1), (3, 0)]


def in_order(odd, mine, other):
    return jnp.concatenate([jnp.where(odd, other, mine), jnp.where(odd, mine, other)], axis=0)


def per_device(recording, traces, footprints, correlation, support):
    comps, rows, cols = footprints.shape
    tiles = rows // TILE
    index = lax.axis_index("rows")
    count = lax.axis_size("rows")
    part = lax.axis_index("tm")
    line = lax.axis_size("tm") == 4
    odd = ((part == 1) | (part == 2)) & line
    where = jnp.stack([index, odd.astype(jnp.int32), jnp.int32(count - 1)]).astype(jnp.int32)
    inside, outside = pairs_of(count, 0), pairs_of(count, 1)
    names = support.T
    field_tiles = tiles_of(footprints)
    spare = comps * tiles - sum(CHUNKS)

    def near(array):
        return lax.ppermute(array, "tm", NEAR)

    def far(array):
        return lax.ppermute(array, "tm", FAR)

    def beside(array):
        return lax.ppermute(array, "rows", outside)

    mine, other = [None, None], [None, None]
    mine[0], other[0] = project(where, names, traces, recording, 0, CHUNKS[:1])
    *_, later = barrier(other[0], traces)
    mine[1], other[1] = project(where, names, later, recording, CHUNKS[0], CHUNKS[1:])
    *_, later = barrier(other[0], field_tiles)
    planes, act, first, pick, late, more = plan(where, support, later, rows, count)
    if line:
        first_received = near(other[0])
        half = [barrier(mine[0] + first_received)[0]]
        later, half[0], planes = barrier(other[1], half[0], planes)
        first_across = far(half[0])
        half.append(barrier(mine[1] + near(later))[0])
        whole = [barrier(half[0] + first_across)[0]]
        half[1], whole[0] = barrier(half[1], whole[0])
        first_back = near(whole[0])
        whole.append(barrier(half[1] + far(half[1]))[0])
        back = [first_back, near(whole[1])]
    else:
        whole, back = lax.psum((mine, other), "tm")
    sums = [barrier(in_order(odd, *barrier(whole[0], back[0])))[0]]
    to_outer = edge_rows(where, sums[0], planes, act, first, correlation)
    outer = beside(to_outer)
    *_, later = barrier(to_outer, planes)
    own, theirs, base, rate = barrier(whole[1], back[1], *prepare(sums[0], later, act))
    prepared = base, pick, late, rate
    sums.append(barrier(in_order(odd, own, theirs))[0])

    def rest():
        mine, other = project(where, names, traces, recording, sum(CHUNKS), (spare,))
        if line:
            half = mine + near(other)
            mine = half + far(half)
            other = near(mine)
        else:
            mine, other = lax.psum((mine, other), "tm")
        field, to_inner, to_outer = step_rows(where, prepared, correlation, sums + [in_order(odd, mine, other)])
        return field, to_inner, jnp.maximum(beside(to_outer), 0.0)

    def enough():
        return tuple(step_rows(where, prepared, correlation, sums))

    field, to_inner, outer_again = lax.cond(more[0] > 0, rest, enough)
    to_inner, outer = barrier(to_inner, outer)
    inner = lax.ppermute(to_inner, "rows", inside)
    result = diffuse(where, more, act, correlation, field, inner, outer, outer_again)
    return from_tiles(result, comps, rows, cols)


def solution(mesh):
    return jax.shard_map(
        per_device,
        mesh=mesh,
        in_specs=(
            P("tm", ("band", "rows"), None),
            P("band", "tm"),
            P(None, ("band", "rows"), None),
            P(("band", "rows"), None),
            P("band", None),
        ),
        out_specs=P(None, ("band", "rows"), None),
        check_vma=False,
    )
```

```python
import functools

import jax
import jax.numpy as jnp
from jax import lax
from jax.sharding import PartitionSpec as P
from jax.experimental import pallas as pl
from jax.experimental.pallas import tpu as pltpu

TILE = 4
PASSES = 4
diffusion_rate = 0.24
step_scale = 0.5
epsilon = 1e-06
FRAME_BLOCK = 128
LANES = 128
GROUP = 8
TERMS = 3
HIGHEST = lax.Precision.HIGHEST
VMEM = pltpu.VMEM
WHOLE = pl.BlockSpec(memory_space=pltpu.VMEM)
SCALARS = pl.BlockSpec(memory_space=pltpu.SMEM)

CHUNKS = (48, 32)


def barrier(*arrays):
    return lax.optimization_barrier(arrays)


def ranges(slots):
    starts = [sum(slots[:chunk]) for chunk in range(len(slots))]
    return [(start, count // 2) for start, count in zip(starts, slots)]


def iota(shape, dim):
    return lax.broadcasted_iota(jnp.int32, shape, dim)


def active(support, tile, axis):
    return jnp.max(jnp.where(support == tile, 1.0, 0.0), axis=axis, keepdims=True)


def project_kernel(first, chunks, where_ref, support_ref, traces_ref, movie_ref, *refs):
    outs, (held_ref, wide_ref, total_ref, gram_ref, arrived) = refs[:-5], refs[-5:]
    comps, frames = traces_ref.shape
    slots = sum(chunks)
    blocks = arrived.shape[0]
    depth = movie_ref.shape[0] // blocks
    rows = movie_ref.shape[0] // frames
    tiles = rows // TILE
    width = depth // rows

    def copy(block):
        part = pl.ds(block * depth, depth)
        return pltpu.make_async_copy(movie_ref.at[part, :], held_ref.at[part, :], arrived.at[block])

    for block in range(blocks):
        copy(block).start()
    spread = jnp.where(iota((width, depth), 0) == iota((width, depth), 1) // rows, 1.0, 0.0).astype(jnp.bfloat16)
    support = support_ref[...]
    upper = jnp.where(iota((comps, comps), 0) < iota((comps, comps), 1), 1.0, 0.0)
    slot = (iota((slots, comps), 0) + first).astype(jnp.float32)
    select = jnp.zeros((slots, comps), jnp.float32)
    before = jnp.zeros((1, 1), jnp.float32)
    base = jnp.full((slots, 1), -rows, jnp.int32)
    for order in range(tiles):
        tile = jnp.where(lax.rem(where_ref[0], 2) == 0, order, tiles - 1 - order)
        act = active(support, where_ref[0] * tiles + tile, 0)
        rank = jnp.dot(jnp.broadcast_to(act, (8, comps)), upper, preferred_element_type=jnp.float32)[0:1] + before
        select = select + jnp.where(slot == rank, act, 0.0)
        after = before + jnp.sum(act, axis=1, keepdims=True)
        here = (slot[:, 0:1] >= before) & (slot[:, 0:1] < after)
        base = jnp.where(here, TILE * tile, base)
        before = after
    select = select.astype(jnp.bfloat16)
    phase = iota((slots, depth), 1) % rows - base
    traces = traces_ref[...]
    chosen = jnp.dot(select, traces, preferred_element_type=jnp.float32).astype(jnp.bfloat16)
    for block in range(blocks):
        repeated = jnp.dot(
            chosen[:, block * width : (block + 1) * width], spread, preferred_element_type=jnp.float32
        )
        for row in range(TILE):
            wide_ref[row * slots : (row + 1) * slots, block * depth : (block + 1) * depth] = jnp.where(
                phase == row, repeated, 0.0
            ).astype(jnp.bfloat16)
    if first == 0:
        gram_ref[...] = lax.dot_general(
            traces, traces, (((1,), (1,)), ((), ())), preferred_element_type=jnp.float32
        )
    for block in range(blocks):
        copy(block).wait()
        part = jnp.dot(
            wide_ref[:, block * depth : (block + 1) * depth],
            held_ref[block * depth : (block + 1) * depth, :],
            preferred_element_type=jnp.float32,
        )
        if block == 0:
            total_ref[...] = part
        else:
            total_ref[...] += part
    odd = where_ref[1]
    for which in range(2):
        mine = odd if which == 0 else 1 - odd
        for chunk, (begin, half) in enumerate(ranges(chunks)):
            ref = outs[2 * chunk + which]
            for row in range(TILE):
                start = pl.multiple_of(row * slots + begin + mine * half, 8)
                ref[row * half : (row + 1) * half, :] = total_ref[pl.ds(start, half), :]
        if first == 0:
            ref = outs[which]
            filled = TILE * chunks[0] // 2
            band = ref.shape[0] - filled
            ref[filled:, :] = jnp.zeros((band, ref.shape[1]), jnp.float32)
            for piece in range(ref.shape[1] // LANES):
                start = pl.multiple_of((2 * piece + mine) * band, 8)
                ref[filled:, piece * LANES : piece * LANES + comps] = gram_ref[pl.ds(start, band), :]


def project(where, support, traces, recording, first, chunks):
    frames, rows, cols = recording.shape
    comps = traces.shape[0]
    slots = sum(chunks)
    shapes = []
    for chunk, (_, half) in enumerate(ranges(chunks)):
        band = comps * LANES // cols // 2 if first == 0 and chunk == 0 else 0
        shapes += [(TILE * half + band, cols)] * 2
    return pl.pallas_call(
        functools.partial(project_kernel, first, chunks),
        name="project",
        in_specs=[SCALARS, WHOLE, WHOLE, pl.BlockSpec(memory_space=pltpu.HBM)],
        out_specs=[WHOLE] * len(shapes),
        out_shape=[jax.ShapeDtypeStruct(shape, jnp.float32) for shape in shapes],
        scratch_shapes=[
            VMEM((frames * rows, cols), jnp.bfloat16),
            VMEM((TILE * slots, frames * rows), jnp.bfloat16),
            VMEM((TILE * slots, cols), jnp.float32),
            VMEM((comps, comps), jnp.float32),
            pltpu.SemaphoreType.DMA((frames // FRAME_BLOCK,)),
        ],
        compiler_params=pltpu.CompilerParams(vmem_limit_bytes=13 << 20),
    )(where, support, traces, recording.reshape(frames * rows, cols))


def tiles_of(array):
    comps, rows, cols = array.shape
    pieces = array.reshape(comps, rows, cols // LANES, LANES).transpose(0, 2, 1, 3)
    return pieces.reshape(comps * rows * cols // LANES, LANES)


def from_tiles(tiles, comps, rows, cols):
    pieces = tiles.reshape(comps, cols // LANES, rows, LANES).transpose(0, 2, 1, 3)
    return pieces.reshape(comps, rows, cols)


def plane_of(tiles_ref, row, comps, rows, cols):
    step = rows * cols // LANES
    pieces = [tiles_ref[pl.ds(piece * rows + row, comps, stride=step), :] for piece in range(cols // LANES)]
    return jnp.concatenate(pieces, axis=1)


def terms_of(packed):
    terms = []
    for _ in range(TERMS):
        term = packed.astype(jnp.bfloat16)
        packed = packed - term.astype(jnp.float32)
        terms.append(term)
    return jnp.concatenate(terms, axis=0)


def slots_of(ref, half, row):
    height = ref.shape[0] // 2
    return [ref[part * height + row * half : part * height + (row + 1) * half, :] for part in range(2)]


def moved(pick, parts):
    terms = terms_of(jnp.concatenate(parts, axis=0))
    return jnp.dot(pick[:, 0 : terms.shape[0]], terms, preferred_element_type=jnp.float32)


def gram_of(sums_ref, comps):
    cols = sums_ref.shape[1]
    band = comps * LANES // cols // 2
    height = sums_ref.shape[0] // 2
    gram = jnp.concatenate(
        [
            sums_ref[(half + 1) * height - band : (half + 1) * height, piece * LANES : piece * LANES + comps]
            for piece in range(cols // LANES)
            for half in range(2)
        ],
        axis=0,
    )
    own = iota(gram.shape, 0) == iota(gram.shape, 1)
    diagonal = jnp.sum(jnp.where(own, gram, 0.0), axis=1, keepdims=True)
    return gram, step_scale / (diagonal + epsilon)


def descend(gram, rate, field, act):
    slope = jnp.dot(gram, field, precision=HIGHEST, preferred_element_type=jnp.float32)
    return jnp.where(act > 0.0, field - rate * slope, 0.0)


def rank_of(act):
    comps = act.shape[0]
    lower = jnp.where(iota((comps, comps), 1) < iota((comps, comps), 0), 1.0, 0.0)
    return jnp.dot(lower, jnp.broadcast_to(act, (comps, LANES)), preferred_element_type=jnp.float32)[:, 0:1]


def term_slots(comps, count, first):
    place = iota((comps, 4 * comps), 1)
    return jnp.where(place < TERMS * count, first + place % count, -1).astype(jnp.float32)


def plan_kernel(
    count, where_ref, support_ref, tiles_ref, planes_ref, act_ref, first_ref, pick_ref, spare_ref, more_ref
):
    rows, comps, cols = planes_ref.shape
    tiles = rows // TILE
    index = where_ref[0]
    main = sum(CHUNKS)
    spare = comps * tiles - main
    support = support_ref[...]
    for row in range(rows):
        planes_ref[row] = plane_of(tiles_ref, row, comps, rows, cols)
    before = jnp.zeros((1, 1), jnp.float32)
    for order in range(tiles):
        tile = jnp.where(lax.rem(index, 2) == 0, order, tiles - 1 - order)
        act = active(support, index * tiles + tile, 1)
        act_ref[tile] = jnp.broadcast_to(act, (comps, LANES))
        rank = before + rank_of(act)
        chosen = pl.ds(pl.multiple_of(tile * comps, comps), comps)
        pick_ref[chosen, :] = jnp.where(term_slots(comps, main, 0) == rank, act, 0.0).astype(jnp.bfloat16)
        spare_ref[chosen, :] = jnp.where(term_slots(comps, spare, main) == rank, act, 0.0).astype(jnp.bfloat16)
        if order == 0:
            first = jnp.where(term_slots(comps, CHUNKS[0], 0) == rank, act, 0.0)
            first_ref[...] = first.astype(jnp.bfloat16)
        before = before + jnp.sum(act, axis=0, keepdims=True)
    over = jnp.full((1, 1), -1.0, jnp.float32)
    for device in range(count):
        held = jnp.zeros((1, 1), jnp.float32)
        for tile in range(tiles):
            in_tile = jnp.sum(active(support, device * tiles + tile, 1), axis=0, keepdims=True)
            over = jnp.maximum(over, in_tile - CHUNKS[0])
            held = held + in_tile
        over = jnp.maximum(over, held - main)
    more_ref[0] = (jnp.max(over) > 0.5).astype(jnp.int32)


def plan(where, support, tiles_in, rows, count):
    comps = support.shape[0]
    cols = tiles_in.shape[0] * LANES // (rows * comps)
    tiles = rows // TILE

    def picks(number):
        return jax.ShapeDtypeStruct((number * comps, 4 * comps), jnp.bfloat16)

    return pl.pallas_call(
        functools.partial(plan_kernel, count),
        name="plan",
        in_specs=[SCALARS] + [WHOLE] * 2,
        out_specs=[WHOLE] * 5 + [SCALARS],
        out_shape=[
            jax.ShapeDtypeStruct((rows, comps, cols), jnp.float32),
            jax.ShapeDtypeStruct((tiles, comps, LANES), jnp.float32),
            picks(1),
            picks(tiles),
            picks(tiles),
            jax.ShapeDtypeStruct((1,), jnp.int32),
        ],
        compiler_params=pltpu.CompilerParams(vmem_limit_bytes=6 << 20),
    )(where, support, tiles_in)


def edge_kernel(where_ref, sums_ref, planes_ref, act_ref, first_ref, correlation_ref, outer_ref):
    rows, comps, cols = planes_ref.shape
    odd = lax.rem(where_ref[0], 2)
    gram, rate = gram_of(sums_ref, comps)
    act = act_ref[odd * (rows // TILE - 1)][:, 0:1]
    for row in range(TILE):
        field = planes_ref[odd * (rows - TILE) + row]
        sums = moved(first_ref, slots_of(sums_ref, CHUNKS[0] // 2, row))
        field = jnp.maximum(descend(gram, rate, field, act) + rate * sums, 0.0)
        outer_ref[row * comps : (row + 1) * comps, :] = field
    outer_ref[TILE * comps :, :] = correlation_ref[...]


def edge_rows(where, sums, planes, act, first, correlation):
    rows, comps, cols = planes.shape
    return pl.pallas_call(
        edge_kernel,
        name="edge_rows",
        in_specs=[SCALARS] + [WHOLE] * 5,
        out_specs=WHOLE,
        out_shape=jax.ShapeDtypeStruct((TILE * comps + rows, cols), jnp.float32),
        compiler_params=pltpu.CompilerParams(vmem_limit_bytes=6 << 20),
    )(where, sums, planes, act, first, correlation)


def prepare_kernel(sums_ref, planes_ref, act_ref, base_ref, rate_ref):
    rows, comps, cols = base_ref.shape
    gram, rate = gram_of(sums_ref, comps)
    rate_ref[...] = jnp.broadcast_to(rate, rate_ref.shape)
    for row in range(rows):
        base_ref[row] = descend(gram, rate, planes_ref[row], act_ref[row // TILE][:, 0:1])


def prepare(sums, planes, act):
    return pl.pallas_call(
        prepare_kernel,
        name="prepare",
        in_specs=[WHOLE] * 3,
        out_specs=[WHOLE] * 2,
        out_shape=[
            jax.ShapeDtypeStruct(planes.shape, jnp.float32),
            jax.ShapeDtypeStruct((planes.shape[1], LANES), jnp.float32),
        ],
        compiler_params=pltpu.CompilerParams(vmem_limit_bytes=6 << 20),
    )(sums, planes, act)


def step_kernel(with_spare, where_ref, base_ref, pick_ref, spare_ref, rate_ref, correlation_ref, *refs):
    refs, outs = refs[: len(CHUNKS) + with_spare], refs[len(CHUNKS) + with_spare :]
    rows, comps, cols = base_ref.shape
    tiles = rows // TILE
    rate = rate_ref[:, 0:1]
    even = lax.rem(where_ref[0], 2) == 0
    for row in range(TILE):
        parts = []
        for ref, (_, half) in zip(refs, ranges(CHUNKS)):
            parts += slots_of(ref, half, row)
        sums = moved(pick_ref, parts)
        if with_spare:
            sums = sums + moved(spare_ref, slots_of(refs[-1], refs[-1].shape[0] // 2 // TILE, row))
        planes = []
        for tile in range(tiles):
            at = tile * TILE + row
            planes.append(jnp.maximum(base_ref[at] + rate * sums[tile * comps : (tile + 1) * comps, :], 0.0))
            outs[0][at] = planes[-1]
        chosen = slice(row * comps, (row + 1) * comps)
        outs[1][chosen, :] = jnp.where(even, planes[-1], planes[0])
        outs[2][chosen, :] = jnp.where(even, planes[0], planes[-1])
    for ref in outs[1:]:
        ref[TILE * comps :, :] = correlation_ref[...]


def step_rows(where, prepared, correlation, sums):
    base = prepared[0]
    rows, comps, cols = base.shape
    spare = len(sums) - len(CHUNKS)
    edge = jax.ShapeDtypeStruct((TILE * comps + rows, cols), jnp.float32)
    return pl.pallas_call(
        functools.partial(step_kernel, spare),
        name="step_rows",
        in_specs=[SCALARS] + [WHOLE] * (5 + len(sums)),
        out_specs=[WHOLE] * 3,
        out_shape=[jax.ShapeDtypeStruct(base.shape, jnp.float32), edge, edge],
        compiler_params=pltpu.CompilerParams(vmem_limit_bytes=6 << 20),
    )(where, *prepared, correlation, *sums)


def diffuse_kernel(
    where_ref,
    more_ref,
    act_ref,
    correlation_ref,
    field_ref,
    inner_ref,
    outer_ref,
    again_ref,
    out_ref,
    done_ref,
    edge_ref,
    weight_ref,
    keep_ref,
    sent,
):
    rows, comps, cols = field_ref.shape
    tiles = rows // TILE
    pieces = cols // LANES
    group = GROUP
    index, last = where_ref[0], where_ref[2]
    odd = lax.rem(index, 2) == 1
    again = more_ref[0] > 0
    has_above = jnp.where(index > 0, 1.0, 0.0)
    has_below = jnp.where(index < last, 1.0, 0.0)
    for row in range(PASSES):
        chosen = slice(row * comps, (row + 1) * comps)
        inner = inner_ref[chosen, :]
        outer = jnp.where(again, again_ref[chosen, :], outer_ref[chosen, :])
        edge_ref[row] = has_above * jnp.where(odd, inner, outer)
        edge_ref[PASSES + row] = has_below * jnp.where(odd, outer, inner)
    inner, outer = inner_ref[PASSES * comps :, :], outer_ref[PASSES * comps :, :]
    parts = (
        (0, (diffusion_rate * has_above) * jnp.where(odd, inner, outer)[rows - PASSES :]),
        (PASSES, diffusion_rate * correlation_ref[...]),
        (PASSES + rows, (diffusion_rate * has_below) * jnp.where(odd, outer, inner)[:PASSES]),
    )
    for first, weight in parts:
        for row in range(weight.shape[0]):
            line = jnp.broadcast_to(weight[row : row + 1, :], (GROUP, cols))
            weight_ref[first + row] = line
            keep_ref[first + row] = 1.0 - 4.0 * line
    lane = iota((group, LANES), 1)
    at_left, at_right = lane == 0, lane == LANES - 1
    nothing = jnp.zeros((group, LANES), jnp.float32)
    total = rows + 2 * PASSES
    size = group * rows * pieces

    def copy(step):
        part = pl.ds(step * size, size)
        return pltpu.make_async_copy(done_ref.at[part, :], out_ref.at[part, :], sent.at[step])

    def relax(step, carry):
        start = pl.multiple_of(step * group, group)

        def load(row):
            if row < PASSES:
                ref, at = edge_ref, row
            elif row < PASSES + rows:
                ref, at = field_ref, row - PASSES
            else:
                ref, at = edge_ref, row - rows
            return [ref[at, pl.ds(start, group), piece * LANES : (piece + 1) * LANES] for piece in range(pieces)]

        def renew(planes, done, at):
            above, center, below = planes[at - 1 : at + 2]
            row = at + done
            to_right = [pltpu.roll(piece, 1, 1) for piece in center]
            to_left = [pltpu.roll(piece, LANES - 1, 1) for piece in center]
            fresh = []
            for piece in range(pieces):
                left = jnp.where(at_left, to_right[piece - 1] if piece > 0 else nothing, to_right[piece])
                right = jnp.where(at_right, to_left[piece + 1] if piece < pieces - 1 else nothing, to_left[piece])
                beside = (above[piece] + below[piece]) + (left + right)
                lanes = slice(piece * LANES, (piece + 1) * LANES)
                fresh.append(keep_ref[row, :, lanes] * center[piece] + weight_ref[row, :, lanes] * beside)
            return fresh

        masks = [act_ref[tile, pl.ds(start, group), :] for tile in range(tiles)]
        planes = [load(row) for row in range(total)]
        for done in range(PASSES):
            planes = [renew(planes, done, at) for at in range(1, len(planes) - 1)]
        for own in range(rows):
            for piece in range(pieces):
                at = pl.ds(step * size + piece * rows + own, group, stride=rows * pieces)
                done_ref[at, :] = planes[own][piece] * masks[own // TILE]
        copy(step).start()
        return carry

    lax.fori_loop(0, comps // group, relax, 0)
    for step in range(comps // group):
        copy(step).wait()


def diffuse(where, more, act, correlation, field, inner, outer, outer_again):
    rows, comps, cols = field.shape
    pieces = cols // LANES
    lines = VMEM((rows + 2 * PASSES, GROUP, cols), jnp.float32)
    shape = (comps * rows * pieces, LANES)
    return pl.pallas_call(
        diffuse_kernel,
        name="diffuse",
        in_specs=[SCALARS] * 2 + [WHOLE] * 6,
        out_specs=pl.BlockSpec(memory_space=pltpu.HBM),
        out_shape=jax.ShapeDtypeStruct(shape, jnp.float32),
        scratch_shapes=[
            VMEM(shape, jnp.float32),
            VMEM((2 * PASSES, comps, cols), jnp.float32),
            lines,
            lines,
            pltpu.SemaphoreType.DMA((comps // GROUP,)),
        ],
        compiler_params=pltpu.CompilerParams(vmem_limit_bytes=8 << 20),
    )(where, more, act, correlation, field, inner, outer, outer_again)


def pairs_of(count, first):
    table = list(range(count))
    for i in range(first, count - 1, 2):
        table[i], table[i + 1] = i + 1, i
    return list(enumerate(table))


NEAR, FAR = pairs_of(4, 0), [(0, 3), (1, 2), (2, 1), (3, 0)]


def in_order(odd, mine, other):
    return jnp.concatenate([jnp.where(odd, other, mine), jnp.where(odd, mine, other)], axis=0)


def per_device(recording, traces, footprints, correlation, support):
    comps, rows, cols = footprints.shape
    tiles = rows // TILE
    index = lax.axis_index("rows")
    count = lax.axis_size("rows")
    part = lax.axis_index("tm")
    line = lax.axis_size("tm") == 4
    odd = ((part == 1) | (part == 2)) & line
    where = jnp.stack([index, odd.astype(jnp.int32), jnp.int32(count - 1)]).astype(jnp.int32)
    inside, outside = pairs_of(count, 0), pairs_of(count, 1)
    names = support.T
    field_tiles = tiles_of(footprints)
    spare = comps * tiles - sum(CHUNKS)

    def near(array):
        return lax.ppermute(array, "tm", NEAR)

    def far(array):
        return lax.ppermute(array, "tm", FAR)

    def beside(array):
        return lax.ppermute(array, "rows", outside)

    mine, other = [None, None], [None, None]
    mine[0], other[0] = project(where, names, traces, recording, 0, CHUNKS[:1])
    if not line:
        mine[1], other[1] = project(where, names, traces, recording, CHUNKS[0], CHUNKS[1:])
    *_, later = barrier(other[0], field_tiles)
    planes, act, first, pick, late, more = plan(where, support, later, rows, count)
    if line:
        first_received = near(other[0])
        half = [barrier(mine[0] + first_received, planes)[0]]
        first_across = far(half[0])
        *_, later = barrier(half[0], traces)
        mine[1], other[1] = project(where, names, later, recording, CHUNKS[0], CHUNKS[1:])
        half.append(barrier(mine[1] + near(other[1]))[0])
        whole = [barrier(half[0] + first_across)[0]]
        half[1], whole[0] = barrier(half[1], whole[0])
        first_back = near(whole[0])
        whole.append(barrier(half[1] + far(half[1]))[0])
        back = [first_back, near(whole[1])]
    else:
        whole, back = lax.psum((mine, other), "tm")
    sums = [barrier(in_order(odd, *barrier(whole[0], back[0])))[0]]
    to_outer = edge_rows(where, sums[0], planes, act, first, correlation)
    outer = beside(to_outer)
    *_, later = barrier(to_outer, planes)
    own, theirs, base, rate = barrier(whole[1], back[1], *prepare(sums[0], later, act))
    prepared = base, pick, late, rate
    sums.append(barrier(in_order(odd, own, theirs))[0])

    def rest():
        mine, other = project(where, names, traces, recording, sum(CHUNKS), (spare,))
        if line:
            half = mine + near(other)
            mine = half + far(half)
            other = near(mine)
        else:
            mine, other = lax.psum((mine, other), "tm")
        field, to_inner, to_outer = step_rows(where, prepared, correlation, sums + [in_order(odd, mine, other)])
        return tuple(jnp.maximum(array, 0.0) for array in (field, to_inner, beside(to_outer)))

    def enough():
        return tuple(step_rows(where, prepared, correlation, sums))

    field, to_inner, outer_again = lax.cond(more[0] > 0, rest, enough)
    to_inner, outer = barrier(to_inner, outer)
    inner = lax.ppermute(to_inner, "rows", inside)
    result = diffuse(where, more, act, correlation, field, inner, outer, outer_again)
    return from_tiles(result, comps, rows, cols)


def solution(mesh):
    return jax.shard_map(
        per_device,
        mesh=mesh,
        in_specs=(
            P("tm", ("band", "rows"), None),
            P("band", "tm"),
            P(None, ("band", "rows"), None),
            P(("band", "rows"), None),
            P("band", None),
        ),
        out_specs=P(None, ("band", "rows"), None),
        check_vma=False,
    )
```

```python
import functools

import jax
import jax.numpy as jnp
from jax import lax
from jax.sharding import PartitionSpec as P
from jax.experimental import pallas as pl
from jax.experimental.pallas import tpu as pltpu

TILE = 4
PASSES = 4
diffusion_rate = 0.24
step_scale = 0.5
epsilon = 1e-06
FRAME_BLOCK = 128
LANES = 128
GROUP = 8
TERMS = 3
HIGHEST = lax.Precision.HIGHEST
VMEM = pltpu.VMEM
WHOLE = pl.BlockSpec(memory_space=pltpu.VMEM)
SCALARS = pl.BlockSpec(memory_space=pltpu.SMEM)

CHUNKS = (48, 32)


def barrier(*arrays):
    return lax.optimization_barrier(arrays)


def ranges(slots):
    starts = [sum(slots[:chunk]) for chunk in range(len(slots))]
    return [(start, count // 2) for start, count in zip(starts, slots)]


def iota(shape, dim):
    return lax.broadcasted_iota(jnp.int32, shape, dim)


def active(support, tile, axis):
    return jnp.max(jnp.where(support == tile, 1.0, 0.0), axis=axis, keepdims=True)


def project_kernel(first, chunks, where_ref, support_ref, traces_ref, movie_ref, *refs):
    outs, (held_ref, wide_ref, total_ref, gram_ref, arrived) = refs[:-5], refs[-5:]
    comps, frames = traces_ref.shape
    slots = sum(chunks)
    blocks = arrived.shape[0]
    depth = movie_ref.shape[0] // blocks
    rows = movie_ref.shape[0] // frames
    tiles = rows // TILE
    width = depth // rows

    def copy(block):
        part = pl.ds(block * depth, depth)
        return pltpu.make_async_copy(movie_ref.at[part, :], held_ref.at[part, :], arrived.at[block])

    for block in range(blocks):
        copy(block).start()
    spread = jnp.where(iota((width, depth), 0) == iota((width, depth), 1) // rows, 1.0, 0.0).astype(jnp.bfloat16)
    support = support_ref[...]
    upper = jnp.where(iota((comps, comps), 0) < iota((comps, comps), 1), 1.0, 0.0)
    slot = (iota((slots, comps), 0) + first).astype(jnp.float32)
    select = jnp.zeros((slots, comps), jnp.float32)
    before = jnp.zeros((1, 1), jnp.float32)
    base = jnp.full((slots, 1), -rows, jnp.int32)
    for order in range(tiles):
        tile = jnp.where(lax.rem(where_ref[0], 2) == 0, order, tiles - 1 - order)
        act = active(support, where_ref[0] * tiles + tile, 0)
        rank = jnp.dot(jnp.broadcast_to(act, (8, comps)), upper, preferred_element_type=jnp.float32)[0:1] + before
        select = select + jnp.where(slot == rank, act, 0.0)
        after = before + jnp.sum(act, axis=1, keepdims=True)
        here = (slot[:, 0:1] >= before) & (slot[:, 0:1] < after)
        base = jnp.where(here, TILE * tile, base)
        before = after
    select = select.astype(jnp.bfloat16)
    phase = iota((slots, depth), 1) % rows - base
    traces = traces_ref[...]
    chosen = jnp.dot(select, traces, preferred_element_type=jnp.float32).astype(jnp.bfloat16)
    for block in range(blocks):
        repeated = jnp.dot(
            chosen[:, block * width : (block + 1) * width], spread, preferred_element_type=jnp.float32
        )
        for row in range(TILE):
            wide_ref[row * slots : (row + 1) * slots, block * depth : (block + 1) * depth] = jnp.where(
                phase == row, repeated, 0.0
            ).astype(jnp.bfloat16)
    if first == 0:
        gram_ref[...] = lax.dot_general(
            traces, traces, (((1,), (1,)), ((), ())), preferred_element_type=jnp.float32
        )
    for block in range(blocks):
        copy(block).wait()
        part = jnp.dot(
            wide_ref[:, block * depth : (block + 1) * depth],
            held_ref[block * depth : (block + 1) * depth, :],
            preferred_element_type=jnp.float32,
        )
        if block == 0:
            total_ref[...] = part
        else:
            total_ref[...] += part
    odd = where_ref[1]
    for which in range(2):
        mine = odd if which == 0 else 1 - odd
        for chunk, (begin, half) in enumerate(ranges(chunks)):
            ref = outs[2 * chunk + which]
            for row in range(TILE):
                start = pl.multiple_of(row * slots + begin + mine * half, 8)
                ref[row * half : (row + 1) * half, :] = total_ref[pl.ds(start, half), :]
        if first == 0:
            ref = outs[which]
            filled = TILE * chunks[0] // 2
            band = ref.shape[0] - filled
            ref[filled:, :] = jnp.zeros((band, ref.shape[1]), jnp.float32)
            for piece in range(ref.shape[1] // LANES):
                start = pl.multiple_of((2 * piece + mine) * band, 8)
                ref[filled:, piece * LANES : piece * LANES + comps] = gram_ref[pl.ds(start, band), :]


def project(where, support, traces, recording, first, chunks):
    frames, rows, cols = recording.shape
    comps = traces.shape[0]
    slots = sum(chunks)
    shapes = []
    for chunk, (_, half) in enumerate(ranges(chunks)):
        band = comps * LANES // cols // 2 if first == 0 and chunk == 0 else 0
        shapes += [(TILE * half + band, cols)] * 2
    return pl.pallas_call(
        functools.partial(project_kernel, first, chunks),
        name="project",
        in_specs=[SCALARS, WHOLE, WHOLE, pl.BlockSpec(memory_space=pltpu.HBM)],
        out_specs=[WHOLE] * len(shapes),
        out_shape=[jax.ShapeDtypeStruct(shape, jnp.float32) for shape in shapes],
        scratch_shapes=[
            VMEM((frames * rows, cols), jnp.bfloat16),
            VMEM((TILE * slots, frames * rows), jnp.bfloat16),
            VMEM((TILE * slots, cols), jnp.float32),
            VMEM((comps, comps), jnp.float32),
            pltpu.SemaphoreType.DMA((frames // FRAME_BLOCK,)),
        ],
        compiler_params=pltpu.CompilerParams(vmem_limit_bytes=13 << 20),
    )(where, support, traces, recording.reshape(frames * rows, cols))


def tiles_of(array):
    comps, rows, cols = array.shape
    pieces = array.reshape(comps, rows, cols // LANES, LANES).transpose(0, 2, 1, 3)
    return pieces.reshape(comps * rows * cols // LANES, LANES)


def from_tiles(tiles, comps, rows, cols):
    pieces = tiles.reshape(comps, cols // LANES, rows, LANES).transpose(0, 2, 1, 3)
    return pieces.reshape(comps, rows, cols)


def plane_of(tiles_ref, row, comps, rows, cols):
    step = rows * cols // LANES
    pieces = [tiles_ref[pl.ds(piece * rows + row, comps, stride=step), :] for piece in range(cols // LANES)]
    return jnp.concatenate(pieces, axis=1)


def terms_of(packed):
    terms = []
    for _ in range(TERMS):
        term = packed.astype(jnp.bfloat16)
        packed = packed - term.astype(jnp.float32)
        terms.append(term)
    return jnp.concatenate(terms, axis=0)


def slots_of(ref, half, row):
    height = ref.shape[0] // 2
    return [ref[part * height + row * half : part * height + (row + 1) * half, :] for part in range(2)]


def moved(pick, parts):
    terms = terms_of(jnp.concatenate(parts, axis=0))
    return jnp.dot(pick[:, 0 : terms.shape[0]], terms, preferred_element_type=jnp.float32)


def gram_of(sums_ref, comps):
    cols = sums_ref.shape[1]
    band = comps * LANES // cols // 2
    height = sums_ref.shape[0] // 2
    gram = jnp.concatenate(
        [
            sums_ref[(half + 1) * height - band : (half + 1) * height, piece * LANES : piece * LANES + comps]
            for piece in range(cols // LANES)
            for half in range(2)
        ],
        axis=0,
    )
    own = iota(gram.shape, 0) == iota(gram.shape, 1)
    diagonal = jnp.sum(jnp.where(own, gram, 0.0), axis=1, keepdims=True)
    return gram, step_scale / (diagonal + epsilon)


def descend(gram, rate, field, act):
    slope = jnp.dot(gram, field, precision=HIGHEST, preferred_element_type=jnp.float32)
    return jnp.where(act > 0.0, field - rate * slope, 0.0)


def rank_of(act):
    comps = act.shape[0]
    lower = jnp.where(iota((comps, comps), 1) < iota((comps, comps), 0), 1.0, 0.0)
    return jnp.dot(lower, jnp.broadcast_to(act, (comps, LANES)), preferred_element_type=jnp.float32)[:, 0:1]


def term_slots(comps, count, first):
    place = iota((comps, 4 * comps), 1)
    return jnp.where(place < TERMS * count, first + place % count, -1).astype(jnp.float32)


def plan_kernel(
    count, where_ref, support_ref, tiles_ref, planes_ref, act_ref, first_ref, pick_ref, spare_ref, more_ref
):
    rows, comps, cols = planes_ref.shape
    tiles = rows // TILE
    index = where_ref[0]
    main = sum(CHUNKS)
    spare = comps * tiles - main
    support = support_ref[...]
    for row in range(rows):
        planes_ref[row] = plane_of(tiles_ref, row, comps, rows, cols)
    before = jnp.zeros((1, 1), jnp.float32)
    for order in range(tiles):
        tile = jnp.where(lax.rem(index, 2) == 0, order, tiles - 1 - order)
        act = active(support, index * tiles + tile, 1)
        act_ref[tile] = jnp.broadcast_to(act, (comps, LANES))
        rank = before + rank_of(act)
        chosen = pl.ds(pl.multiple_of(tile * comps, comps), comps)
        pick_ref[chosen, :] = jnp.where(term_slots(comps, main, 0) == rank, act, 0.0).astype(jnp.bfloat16)
        spare_ref[chosen, :] = jnp.where(term_slots(comps, spare, main) == rank, act, 0.0).astype(jnp.bfloat16)
        if order == 0:
            first = jnp.where(term_slots(comps, CHUNKS[0], 0) == rank, act, 0.0)
            first_ref[...] = first.astype(jnp.bfloat16)
        before = before + jnp.sum(act, axis=0, keepdims=True)
    over = jnp.full((1, 1), -1.0, jnp.float32)
    for device in range(count):
        held = jnp.zeros((1, 1), jnp.float32)
        for tile in range(tiles):
            in_tile = jnp.sum(active(support, device * tiles + tile, 1), axis=0, keepdims=True)
            over = jnp.maximum(over, in_tile - CHUNKS[0])
            held = held + in_tile
        over = jnp.maximum(over, held - main)
    more_ref[0] = (jnp.max(over) > 0.5).astype(jnp.int32)


def plan(where, support, tiles_in, rows, count):
    comps = support.shape[0]
    cols = tiles_in.shape[0] * LANES // (rows * comps)
    tiles = rows // TILE

    def picks(number):
        return jax.ShapeDtypeStruct((number * comps, 4 * comps), jnp.bfloat16)

    return pl.pallas_call(
        functools.partial(plan_kernel, count),
        name="plan",
        in_specs=[SCALARS] + [WHOLE] * 2,
        out_specs=[WHOLE] * 5 + [SCALARS],
        out_shape=[
            jax.ShapeDtypeStruct((rows, comps, cols), jnp.float32),
            jax.ShapeDtypeStruct((tiles, comps, LANES), jnp.float32),
            picks(1),
            picks(tiles),
            picks(tiles),
            jax.ShapeDtypeStruct((1,), jnp.int32),
        ],
        compiler_params=pltpu.CompilerParams(vmem_limit_bytes=6 << 20),
    )(where, support, tiles_in)


def edge_kernel(where_ref, sums_ref, planes_ref, act_ref, first_ref, correlation_ref, outer_ref):
    rows, comps, cols = planes_ref.shape
    odd = lax.rem(where_ref[0], 2)
    gram, rate = gram_of(sums_ref, comps)
    act = act_ref[odd * (rows // TILE - 1)][:, 0:1]
    for row in range(TILE):
        field = planes_ref[odd * (rows - TILE) + row]
        sums = moved(first_ref, slots_of(sums_ref, CHUNKS[0] // 2, row))
        field = jnp.maximum(descend(gram, rate, field, act) + rate * sums, 0.0)
        outer_ref[row * comps : (row + 1) * comps, :] = field
    outer_ref[TILE * comps :, :] = correlation_ref[...]


def edge_rows(where, sums, planes, act, first, correlation):
    rows, comps, cols = planes.shape
    return pl.pallas_call(
        edge_kernel,
        name="edge_rows",
        in_specs=[SCALARS] + [WHOLE] * 5,
        out_specs=WHOLE,
        out_shape=jax.ShapeDtypeStruct((TILE * comps + rows, cols), jnp.float32),
        compiler_params=pltpu.CompilerParams(vmem_limit_bytes=6 << 20),
    )(where, sums, planes, act, first, correlation)


def prepare_kernel(sums_ref, planes_ref, act_ref, base_ref, rate_ref):
    rows, comps, cols = base_ref.shape
    gram, rate = gram_of(sums_ref, comps)
    rate_ref[...] = jnp.broadcast_to(rate, rate_ref.shape)
    for row in range(rows):
        base_ref[row] = descend(gram, rate, planes_ref[row], act_ref[row // TILE][:, 0:1])


def prepare(sums, planes, act):
    return pl.pallas_call(
        prepare_kernel,
        name="prepare",
        in_specs=[WHOLE] * 3,
        out_specs=[WHOLE] * 2,
        out_shape=[
            jax.ShapeDtypeStruct(planes.shape, jnp.float32),
            jax.ShapeDtypeStruct((planes.shape[1], LANES), jnp.float32),
        ],
        compiler_params=pltpu.CompilerParams(vmem_limit_bytes=6 << 20),
    )(sums, planes, act)


def step_kernel(with_spare, where_ref, base_ref, pick_ref, spare_ref, rate_ref, correlation_ref, *refs):
    refs, outs = refs[: len(CHUNKS) + with_spare], refs[len(CHUNKS) + with_spare :]
    rows, comps, cols = base_ref.shape
    tiles = rows // TILE
    rate = rate_ref[:, 0:1]
    even = lax.rem(where_ref[0], 2) == 0
    for row in range(TILE):
        parts = []
        for ref, (_, half) in zip(refs, ranges(CHUNKS)):
            parts += slots_of(ref, half, row)
        sums = moved(pick_ref, parts)
        if with_spare:
            sums = sums + moved(spare_ref, slots_of(refs[-1], refs[-1].shape[0] // 2 // TILE, row))
        planes = []
        for tile in range(tiles):
            at = tile * TILE + row
            planes.append(jnp.maximum(base_ref[at] + rate * sums[tile * comps : (tile + 1) * comps, :], 0.0))
            outs[0][at] = planes[-1]
        chosen = slice(row * comps, (row + 1) * comps)
        outs[1][chosen, :] = jnp.where(even, planes[-1], planes[0])
        outs[2][chosen, :] = jnp.where(even, planes[0], planes[-1])
    for ref in outs[1:]:
        ref[TILE * comps :, :] = correlation_ref[...]


def step_rows(where, prepared, correlation, sums):
    base = prepared[0]
    rows, comps, cols = base.shape
    spare = len(sums) - len(CHUNKS)
    edge = jax.ShapeDtypeStruct((TILE * comps + rows, cols), jnp.float32)
    return pl.pallas_call(
        functools.partial(step_kernel, spare),
        name="step_rows",
        in_specs=[SCALARS] + [WHOLE] * (5 + len(sums)),
        out_specs=[WHOLE] * 3,
        out_shape=[jax.ShapeDtypeStruct(base.shape, jnp.float32), edge, edge],
        compiler_params=pltpu.CompilerParams(vmem_limit_bytes=6 << 20),
    )(where, *prepared, correlation, *sums)


def diffuse_kernel(
    where_ref,
    more_ref,
    act_ref,
    correlation_ref,
    field_ref,
    inner_ref,
    outer_ref,
    again_ref,
    out_ref,
    done_ref,
    edge_ref,
    weight_ref,
    keep_ref,
    sent,
):
    rows, comps, cols = field_ref.shape
    tiles = rows // TILE
    pieces = cols // LANES
    group = GROUP
    index, last = where_ref[0], where_ref[2]
    odd = lax.rem(index, 2) == 1
    again = more_ref[0] > 0
    has_above = jnp.where(index > 0, 1.0, 0.0)
    has_below = jnp.where(index < last, 1.0, 0.0)

    inner_at = jnp.where(odd, 0, PASSES)
    outer_at = PASSES - inner_at
    has_outer = jnp.where(odd, has_below, has_above)
    has_inner = jnp.where(odd, has_above, has_below)
    for row in range(PASSES):
        chosen = slice(row * comps, (row + 1) * comps)
        edge_ref[inner_at + row] = has_inner * inner_ref[chosen, :]
        edge_ref[outer_at + row] = has_outer * outer_ref[chosen, :]

    @pl.when(again)
    def _():
        for row in range(PASSES):
            edge_ref[outer_at + row] = has_outer * again_ref[row * comps : (row + 1) * comps, :]

    inner, outer = inner_ref[PASSES * comps :, :], outer_ref[PASSES * comps :, :]
    parts = (
        (0, (diffusion_rate * has_above) * jnp.where(odd, inner, outer)[rows - PASSES :]),
        (PASSES, diffusion_rate * correlation_ref[...]),
        (PASSES + rows, (diffusion_rate * has_below) * jnp.where(odd, outer, inner)[:PASSES]),
    )
    for first, weight in parts:
        for row in range(weight.shape[0]):
            line = jnp.broadcast_to(weight[row : row + 1, :], (GROUP, cols))
            weight_ref[first + row] = line
            keep_ref[first + row] = 1.0 - 4.0 * line
    lane = iota((group, LANES), 1)
    at_left, at_right = lane == 0, lane == LANES - 1
    nothing = jnp.zeros((group, LANES), jnp.float32)
    total = rows + 2 * PASSES
    size = group * rows * pieces

    def copy(step):
        part = pl.ds(step * size, size)
        return pltpu.make_async_copy(done_ref.at[part, :], out_ref.at[part, :], sent.at[step])

    def relax(step, carry):
        start = pl.multiple_of(step * group, group)

        def load(row):
            if row < PASSES:
                ref, at = edge_ref, row
            elif row < PASSES + rows:
                ref, at = field_ref, row - PASSES
            else:
                ref, at = edge_ref, row - rows
            return [ref[at, pl.ds(start, group), piece * LANES : (piece + 1) * LANES] for piece in range(pieces)]

        def renew(planes, done, at):
            above, center, below = planes[at - 1 : at + 2]
            row = at + done
            to_right = [pltpu.roll(piece, 1, 1) for piece in center]
            to_left = [pltpu.roll(piece, LANES - 1, 1) for piece in center]
            fresh = []
            for piece in range(pieces):
                left = jnp.where(at_left, to_right[piece - 1] if piece > 0 else nothing, to_right[piece])
                right = jnp.where(at_right, to_left[piece + 1] if piece < pieces - 1 else nothing, to_left[piece])
                beside = (above[piece] + below[piece]) + (left + right)
                lanes = slice(piece * LANES, (piece + 1) * LANES)
                fresh.append(keep_ref[row, :, lanes] * center[piece] + weight_ref[row, :, lanes] * beside)
            return fresh

        masks = [act_ref[tile, pl.ds(start, group), :] for tile in range(tiles)]
        planes = [load(row) for row in range(total)]
        for done in range(PASSES):
            planes = [renew(planes, done, at) for at in range(1, len(planes) - 1)]
        for own in range(rows):
            for piece in range(pieces):
                at = pl.ds(step * size + piece * rows + own, group, stride=rows * pieces)
                done_ref[at, :] = planes[own][piece] * masks[own // TILE]
        copy(step).start()
        return carry

    lax.fori_loop(0, comps // group, relax, 0, unroll=2)
    for step in range(comps // group):
        copy(step).wait()


def diffuse(where, more, act, correlation, field, inner, outer, outer_again):
    rows, comps, cols = field.shape
    pieces = cols // LANES
    lines = VMEM((rows + 2 * PASSES, GROUP, cols), jnp.float32)
    shape = (comps * rows * pieces, LANES)
    return pl.pallas_call(
        diffuse_kernel,
        name="diffuse",
        in_specs=[SCALARS] * 2 + [WHOLE] * 6,
        out_specs=pl.BlockSpec(memory_space=pltpu.HBM),
        out_shape=jax.ShapeDtypeStruct(shape, jnp.float32),
        scratch_shapes=[
            VMEM(shape, jnp.float32),
            VMEM((2 * PASSES, comps, cols), jnp.float32),
            lines,
            lines,
            pltpu.SemaphoreType.DMA((comps // GROUP,)),
        ],
        compiler_params=pltpu.CompilerParams(vmem_limit_bytes=8 << 20),
    )(where, more, act, correlation, field, inner, outer, outer_again)


def pairs_of(count, first):
    table = list(range(count))
    for i in range(first, count - 1, 2):
        table[i], table[i + 1] = i + 1, i
    return list(enumerate(table))


NEAR, FAR = pairs_of(4, 0), [(0, 3), (1, 2), (2, 1), (3, 0)]


def in_order(odd, mine, other):
    return jnp.concatenate([jnp.where(odd, other, mine), jnp.where(odd, mine, other)], axis=0)


def per_device(recording, traces, footprints, correlation, support):
    comps, rows, cols = footprints.shape
    tiles = rows // TILE
    index = lax.axis_index("rows")
    count = lax.axis_size("rows")
    part = lax.axis_index("tm")
    line = lax.axis_size("tm") == 4
    odd = ((part == 1) | (part == 2)) & line
    where = jnp.stack([index, odd.astype(jnp.int32), jnp.int32(count - 1)]).astype(jnp.int32)
    inside, outside = pairs_of(count, 0), pairs_of(count, 1)
    names = support.T
    field_tiles = tiles_of(footprints)
    spare = comps * tiles - sum(CHUNKS)

    def near(array):
        return lax.ppermute(array, "tm", NEAR)

    def far(array):
        return lax.ppermute(array, "tm", FAR)

    def beside(array):
        return lax.ppermute(array, "rows", outside)

    mine, other = [None, None], [None, None]
    mine[0], other[0] = project(where, names, traces, recording, 0, CHUNKS[:1])
    if not line:
        mine[1], other[1] = project(where, names, traces, recording, CHUNKS[0], CHUNKS[1:])
    *_, later = barrier(other[0], field_tiles)
    planes, act, first, pick, late, more = plan(where, support, later, rows, count)
    if line:
        first_received = near(other[0])
        half = [barrier(mine[0] + first_received, planes)[0]]
        first_across = far(half[0])
        *_, later = barrier(half[0], traces)
        mine[1], other[1] = project(where, names, later, recording, CHUNKS[0], CHUNKS[1:])
        half.append(barrier(mine[1] + near(other[1]))[0])
        whole = [barrier(half[0] + first_across)[0]]
        half[1], whole[0] = barrier(half[1], whole[0])
        first_back = near(whole[0])
        whole.append(barrier(half[1] + far(half[1]))[0])
        back = [first_back, near(whole[1])]
    else:
        whole, back = lax.psum((mine, other), "tm")
    sums = [barrier(in_order(odd, *barrier(whole[0], back[0])))[0]]
    to_outer = edge_rows(where, sums[0], planes, act, first, correlation)
    outer = beside(to_outer)
    *_, later = barrier(to_outer, planes)
    own, theirs, base, rate = barrier(whole[1], back[1], *prepare(sums[0], later, act))
    prepared = base, pick, late, rate
    sums.append(barrier(in_order(odd, own, theirs))[0])

    def rest():
        mine, other = project(where, names, traces, recording, sum(CHUNKS), (spare,))
        if line:
            half = mine + near(other)
            mine = half + far(half)
            other = near(mine)
        else:
            mine, other = lax.psum((mine, other), "tm")
        field, to_inner, to_outer = step_rows(where, prepared, correlation, sums + [in_order(odd, mine, other)])
        return tuple(jnp.maximum(array, 0.0) for array in (field, to_inner, beside(to_outer)))

    def enough():
        return tuple(step_rows(where, prepared, correlation, sums))

    field, to_inner, outer_again = lax.cond(more[0] > 0, rest, enough)
    to_inner, outer = barrier(to_inner, outer)
    inner = lax.ppermute(to_inner, "rows", inside)
    result = diffuse(where, more, act, correlation, field, inner, outer, outer_again)
    return from_tiles(result, comps, rows, cols)


def solution(mesh):
    return jax.shard_map(
        per_device,
        mesh=mesh,
        in_specs=(
            P("tm", ("band", "rows"), None),
            P("band", "tm"),
            P(None, ("band", "rows"), None),
            P(("band", "rows"), None),
            P("band", None),
        ),
        out_specs=P(None, ("band", "rows"), None),
        check_vma=False,
    )
```

```python
import functools

import jax
import jax.numpy as jnp
from jax import lax
from jax.sharding import PartitionSpec as P
from jax.experimental import pallas as pl
from jax.experimental.pallas import tpu as pltpu

TILE = 4
PASSES = 4
diffusion_rate = 0.24
step_scale = 0.5
epsilon = 1e-06
FRAME_BLOCK = 128
LANES = 128
GROUP = 8
TERMS = 3
HIGHEST = lax.Precision.HIGHEST
VMEM = pltpu.VMEM
WHOLE = pl.BlockSpec(memory_space=pltpu.VMEM)
SCALARS = pl.BlockSpec(memory_space=pltpu.SMEM)

CHUNKS = (48, 32)


def barrier(*arrays):
    return lax.optimization_barrier(arrays)


def ranges(slots):
    starts = [sum(slots[:chunk]) for chunk in range(len(slots))]
    return [(start, count // 2) for start, count in zip(starts, slots)]


def iota(shape, dim):
    return lax.broadcasted_iota(jnp.int32, shape, dim)


def active(support, tile, axis):
    return jnp.max(jnp.where(support == tile, 1.0, 0.0), axis=axis, keepdims=True)


def project_kernel(first, chunks, where_ref, support_ref, traces_ref, movie_ref, *refs):
    outs, (held_ref, wide_ref, total_ref, gram_ref, arrived) = refs[:-5], refs[-5:]
    comps, frames = traces_ref.shape
    slots = sum(chunks)
    blocks = arrived.shape[0]
    depth = movie_ref.shape[0] // blocks
    rows = movie_ref.shape[0] // frames
    tiles = rows // TILE
    width = depth // rows

    def copy(block):
        part = pl.ds(block * depth, depth)
        return pltpu.make_async_copy(movie_ref.at[part, :], held_ref.at[part, :], arrived.at[block])

    for block in range(blocks):
        copy(block).start()
    spread = jnp.where(iota((width, depth), 0) == iota((width, depth), 1) // rows, 1.0, 0.0).astype(jnp.bfloat16)
    support = support_ref[...]
    upper = jnp.where(iota((comps, comps), 0) < iota((comps, comps), 1), 1.0, 0.0)
    slot = (iota((slots, comps), 0) + first).astype(jnp.float32)
    select = jnp.zeros((slots, comps), jnp.float32)
    before = jnp.zeros((1, 1), jnp.float32)
    base = jnp.full((slots, 1), -rows, jnp.int32)
    for order in range(tiles):
        tile = jnp.where(lax.rem(where_ref[0], 2) == 0, order, tiles - 1 - order)
        act = active(support, where_ref[0] * tiles + tile, 0)
        rank = jnp.dot(jnp.broadcast_to(act, (8, comps)), upper, preferred_element_type=jnp.float32)[0:1] + before
        select = select + jnp.where(slot == rank, act, 0.0)
        after = before + jnp.sum(act, axis=1, keepdims=True)
        here = (slot[:, 0:1] >= before) & (slot[:, 0:1] < after)
        base = jnp.where(here, TILE * tile, base)
        before = after
    select = select.astype(jnp.bfloat16)
    phase = iota((slots, depth), 1) % rows - base
    traces = traces_ref[...]
    chosen = jnp.dot(select, traces, preferred_element_type=jnp.float32).astype(jnp.bfloat16)
    for block in range(blocks):
        repeated = jnp.dot(
            chosen[:, block * width : (block + 1) * width], spread, preferred_element_type=jnp.float32
        )
        for row in range(TILE):
            wide_ref[row * slots : (row + 1) * slots, block * depth : (block + 1) * depth] = jnp.where(
                phase == row, repeated, 0.0
            ).astype(jnp.bfloat16)
    if first == 0:
        gram_ref[...] = lax.dot_general(
            traces, traces, (((1,), (1,)), ((), ())), preferred_element_type=jnp.float32
        )
    for block in range(blocks):
        copy(block).wait()
        part = jnp.dot(
            wide_ref[:, block * depth : (block + 1) * depth],
            held_ref[block * depth : (block + 1) * depth, :],
            preferred_element_type=jnp.float32,
        )
        if block == 0:
            total_ref[...] = part
        else:
            total_ref[...] += part
    odd = where_ref[1]
    for which in range(2):
        mine = odd if which == 0 else 1 - odd
        for chunk, (begin, half) in enumerate(ranges(chunks)):
            ref = outs[2 * chunk + which]
            for row in range(TILE):
                start = pl.multiple_of(row * slots + begin + mine * half, 8)
                ref[row * half : (row + 1) * half, :] = total_ref[pl.ds(start, half), :]
        if first == 0:
            ref = outs[which]
            filled = TILE * chunks[0] // 2
            band = ref.shape[0] - filled
            ref[filled:, :] = jnp.zeros((band, ref.shape[1]), jnp.float32)
            for piece in range(ref.shape[1] // LANES):
                start = pl.multiple_of((2 * piece + mine) * band, 8)
                ref[filled:, piece * LANES : piece * LANES + comps] = gram_ref[pl.ds(start, band), :]


def project(where, support, traces, recording, first, chunks):
    frames, rows, cols = recording.shape
    comps = traces.shape[0]
    slots = sum(chunks)
    shapes = []
    for chunk, (_, half) in enumerate(ranges(chunks)):
        band = comps * LANES // cols // 2 if first == 0 and chunk == 0 else 0
        shapes += [(TILE * half + band, cols)] * 2
    return pl.pallas_call(
        functools.partial(project_kernel, first, chunks),
        name="project",
        in_specs=[SCALARS, WHOLE, WHOLE, pl.BlockSpec(memory_space=pltpu.HBM)],
        out_specs=[WHOLE] * len(shapes),
        out_shape=[jax.ShapeDtypeStruct(shape, jnp.float32) for shape in shapes],
        scratch_shapes=[
            VMEM((frames * rows, cols), jnp.bfloat16),
            VMEM((TILE * slots, frames * rows), jnp.bfloat16),
            VMEM((TILE * slots, cols), jnp.float32),
            VMEM((comps, comps), jnp.float32),
            pltpu.SemaphoreType.DMA((frames // FRAME_BLOCK,)),
        ],
        compiler_params=pltpu.CompilerParams(vmem_limit_bytes=13 << 20),
    )(where, support, traces, recording.reshape(frames * rows, cols))


def tiles_of(array):
    comps, rows, cols = array.shape
    pieces = array.reshape(comps, rows, cols // LANES, LANES).transpose(0, 2, 1, 3)
    return pieces.reshape(comps * rows * cols // LANES, LANES)


def from_tiles(tiles, comps, rows, cols):
    pieces = tiles.reshape(comps, cols // LANES, rows, LANES).transpose(0, 2, 1, 3)
    return pieces.reshape(comps, rows, cols)


def plane_of(tiles_ref, row, comps, rows, cols):
    step = rows * cols // LANES
    pieces = [tiles_ref[pl.ds(piece * rows + row, comps, stride=step), :] for piece in range(cols // LANES)]
    return jnp.concatenate(pieces, axis=1)


def terms_of(packed):
    terms = []
    for _ in range(TERMS):
        term = packed.astype(jnp.bfloat16)
        packed = packed - term.astype(jnp.float32)
        terms.append(term)
    return jnp.concatenate(terms, axis=0)


def slots_of(ref, half, row):
    height = ref.shape[0] // 2
    return [ref[part * height + row * half : part * height + (row + 1) * half, :] for part in range(2)]


def moved(pick, parts):
    terms = terms_of(jnp.concatenate(parts, axis=0))
    return jnp.dot(pick[:, 0 : terms.shape[0]], terms, preferred_element_type=jnp.float32)


def gram_of(sums_ref, comps):
    cols = sums_ref.shape[1]
    band = comps * LANES // cols // 2
    height = sums_ref.shape[0] // 2
    gram = jnp.concatenate(
        [
            sums_ref[(half + 1) * height - band : (half + 1) * height, piece * LANES : piece * LANES + comps]
            for piece in range(cols // LANES)
            for half in range(2)
        ],
        axis=0,
    )
    own = iota(gram.shape, 0) == iota(gram.shape, 1)
    diagonal = jnp.sum(jnp.where(own, gram, 0.0), axis=1, keepdims=True)
    return gram, step_scale / (diagonal + epsilon)


def descend(gram, rate, field, act):
    slope = jnp.dot(gram, field, precision=HIGHEST, preferred_element_type=jnp.float32)
    return jnp.where(act > 0.0, field - rate * slope, 0.0)


def rank_of(act):
    comps = act.shape[0]
    lower = jnp.where(iota((comps, comps), 1) < iota((comps, comps), 0), 1.0, 0.0)
    return jnp.dot(lower, jnp.broadcast_to(act, (comps, LANES)), preferred_element_type=jnp.float32)[:, 0:1]


def term_slots(comps, count, first):
    place = iota((comps, 4 * comps), 1)
    return jnp.where(place < TERMS * count, first + place % count, -1).astype(jnp.float32)


def plan_kernel(
    count, where_ref, support_ref, tiles_ref, planes_ref, act_ref, first_ref, pick_ref, spare_ref, more_ref
):
    rows, comps, cols = planes_ref.shape
    tiles = rows // TILE
    index = where_ref[0]
    main = sum(CHUNKS)
    spare = comps * tiles - main
    support = support_ref[...]
    for row in range(rows):
        planes_ref[row] = plane_of(tiles_ref, row, comps, rows, cols)
    before = jnp.zeros((1, 1), jnp.float32)
    for order in range(tiles):
        tile = jnp.where(lax.rem(index, 2) == 0, order, tiles - 1 - order)
        act = active(support, index * tiles + tile, 1)
        act_ref[tile] = jnp.broadcast_to(act, (comps, LANES))
        rank = before + rank_of(act)
        chosen = pl.ds(pl.multiple_of(tile * comps, comps), comps)
        pick_ref[chosen, :] = jnp.where(term_slots(comps, main, 0) == rank, act, 0.0).astype(jnp.bfloat16)
        spare_ref[chosen, :] = jnp.where(term_slots(comps, spare, main) == rank, act, 0.0).astype(jnp.bfloat16)
        if order == 0:
            first = jnp.where(term_slots(comps, CHUNKS[0], 0) == rank, act, 0.0)
            first_ref[...] = first.astype(jnp.bfloat16)
        before = before + jnp.sum(act, axis=0, keepdims=True)
    over = jnp.full((1, 1), -1.0, jnp.float32)
    for device in range(count):
        held = jnp.zeros((1, 1), jnp.float32)
        for tile in range(tiles):
            in_tile = jnp.sum(active(support, device * tiles + tile, 1), axis=0, keepdims=True)
            over = jnp.maximum(over, in_tile - CHUNKS[0])
            held = held + in_tile
        over = jnp.maximum(over, held - main)
    more_ref[0] = (jnp.max(over) > 0.5).astype(jnp.int32)


def plan(where, support, tiles_in, rows, count):
    comps = support.shape[0]
    cols = tiles_in.shape[0] * LANES // (rows * comps)
    tiles = rows // TILE

    def picks(number):
        return jax.ShapeDtypeStruct((number * comps, 4 * comps), jnp.bfloat16)

    return pl.pallas_call(
        functools.partial(plan_kernel, count),
        name="plan",
        in_specs=[SCALARS] + [WHOLE] * 2,
        out_specs=[WHOLE] * 5 + [SCALARS],
        out_shape=[
            jax.ShapeDtypeStruct((rows, comps, cols), jnp.float32),
            jax.ShapeDtypeStruct((tiles, comps, LANES), jnp.float32),
            picks(1),
            picks(tiles),
            picks(tiles),
            jax.ShapeDtypeStruct((1,), jnp.int32),
        ],
        compiler_params=pltpu.CompilerParams(vmem_limit_bytes=6 << 20),
    )(where, support, tiles_in)


def edge_kernel(where_ref, sums_ref, planes_ref, act_ref, first_ref, correlation_ref, outer_ref):
    rows, comps, cols = planes_ref.shape
    odd = lax.rem(where_ref[0], 2)
    gram, rate = gram_of(sums_ref, comps)
    act = act_ref[odd * (rows // TILE - 1)][:, 0:1]
    for row in range(TILE):
        field = planes_ref[odd * (rows - TILE) + row]
        sums = moved(first_ref, slots_of(sums_ref, CHUNKS[0] // 2, row))
        field = jnp.maximum(descend(gram, rate, field, act) + rate * sums, 0.0)
        outer_ref[row * comps : (row + 1) * comps, :] = field
    outer_ref[TILE * comps :, :] = correlation_ref[...]


def edge_rows(where, sums, planes, act, first, correlation):
    rows, comps, cols = planes.shape
    return pl.pallas_call(
        edge_kernel,
        name="edge_rows",
        in_specs=[SCALARS] + [WHOLE] * 5,
        out_specs=WHOLE,
        out_shape=jax.ShapeDtypeStruct((TILE * comps + rows, cols), jnp.float32),
        compiler_params=pltpu.CompilerParams(vmem_limit_bytes=6 << 20),
    )(where, sums, planes, act, first, correlation)


def prepare_kernel(sums_ref, planes_ref, act_ref, base_ref, rate_ref):
    rows, comps, cols = base_ref.shape
    gram, rate = gram_of(sums_ref, comps)
    rate_ref[...] = jnp.broadcast_to(rate, rate_ref.shape)
    for row in range(rows):
        base_ref[row] = descend(gram, rate, planes_ref[row], act_ref[row // TILE][:, 0:1])


def prepare(sums, planes, act):
    return pl.pallas_call(
        prepare_kernel,
        name="prepare",
        in_specs=[WHOLE] * 3,
        out_specs=[WHOLE] * 2,
        out_shape=[
            jax.ShapeDtypeStruct(planes.shape, jnp.float32),
            jax.ShapeDtypeStruct((planes.shape[1], LANES), jnp.float32),
        ],
        compiler_params=pltpu.CompilerParams(vmem_limit_bytes=6 << 20),
    )(sums, planes, act)


def step_kernel(with_spare, where_ref, base_ref, pick_ref, spare_ref, rate_ref, correlation_ref, *refs):
    refs, outs = refs[: len(CHUNKS) + with_spare], refs[len(CHUNKS) + with_spare :]
    rows, comps, cols = base_ref.shape
    tiles = rows // TILE
    rate = rate_ref[:, 0:1]
    even = lax.rem(where_ref[0], 2) == 0
    for row in range(TILE):
        parts = []
        for ref, (_, half) in zip(refs, ranges(CHUNKS)):
            parts += slots_of(ref, half, row)
        sums = moved(pick_ref, parts)
        if with_spare:
            sums = sums + moved(spare_ref, slots_of(refs[-1], refs[-1].shape[0] // 2 // TILE, row))
        planes = []
        for tile in range(tiles):
            at = tile * TILE + row
            planes.append(jnp.maximum(base_ref[at] + rate * sums[tile * comps : (tile + 1) * comps, :], 0.0))
            outs[0][at] = planes[-1]
        chosen = slice(row * comps, (row + 1) * comps)
        outs[1][chosen, :] = jnp.where(even, planes[-1], planes[0])
        outs[2][chosen, :] = jnp.where(even, planes[0], planes[-1])
    for ref in outs[1:]:
        ref[TILE * comps :, :] = correlation_ref[...]


def step_rows(where, prepared, correlation, sums):
    base = prepared[0]
    rows, comps, cols = base.shape
    spare = len(sums) - len(CHUNKS)
    edge = jax.ShapeDtypeStruct((TILE * comps + rows, cols), jnp.float32)
    return pl.pallas_call(
        functools.partial(step_kernel, spare),
        name="step_rows",
        in_specs=[SCALARS] + [WHOLE] * (5 + len(sums)),
        out_specs=[WHOLE] * 3,
        out_shape=[jax.ShapeDtypeStruct(base.shape, jnp.float32), edge, edge],
        compiler_params=pltpu.CompilerParams(vmem_limit_bytes=6 << 20),
    )(where, *prepared, correlation, *sums)


def diffuse_kernel(
    where_ref,
    more_ref,
    act_ref,
    correlation_ref,
    field_ref,
    inner_ref,
    outer_ref,
    again_ref,
    out_ref,
    done_ref,
    edge_ref,
    weight_ref,
    keep_ref,
    sent,
):
    rows, comps, cols = field_ref.shape
    tiles = rows // TILE
    pieces = cols // LANES
    group = GROUP
    index, last = where_ref[0], where_ref[2]
    odd = lax.rem(index, 2) == 1
    again = more_ref[0] > 0
    has_above = jnp.where(index > 0, 1.0, 0.0)
    has_below = jnp.where(index < last, 1.0, 0.0)

    inner_at = jnp.where(odd, 0, PASSES)
    outer_at = PASSES - inner_at
    has_outer = jnp.where(odd, has_below, has_above)
    has_inner = jnp.where(odd, has_above, has_below)
    for row in range(PASSES):
        chosen = slice(row * comps, (row + 1) * comps)
        edge_ref[inner_at + row] = has_inner * inner_ref[chosen, :]
        edge_ref[outer_at + row] = has_outer * outer_ref[chosen, :]

    @pl.when(again)
    def _():
        for row in range(PASSES):
            edge_ref[outer_at + row] = has_outer * again_ref[row * comps : (row + 1) * comps, :]

    inner, outer = inner_ref[PASSES * comps :, :], outer_ref[PASSES * comps :, :]
    parts = (
        (0, (diffusion_rate * has_above) * jnp.where(odd, inner, outer)[rows - PASSES :]),
        (PASSES, diffusion_rate * correlation_ref[...]),
        (PASSES + rows, (diffusion_rate * has_below) * jnp.where(odd, outer, inner)[:PASSES]),
    )
    for first, weight in parts:
        for row in range(weight.shape[0]):
            line = jnp.broadcast_to(weight[row : row + 1, :], (GROUP, cols))
            weight_ref[first + row] = line
            keep_ref[first + row] = 1.0 - 4.0 * line
    lane = iota((group, LANES), 1)
    at_left, at_right = lane == 0, lane == LANES - 1
    nothing = jnp.zeros((group, LANES), jnp.float32)
    total = rows + 2 * PASSES
    size = group * rows * pieces

    def copy(step):
        part = pl.ds(step * size, size)
        return pltpu.make_async_copy(done_ref.at[part, :], out_ref.at[part, :], sent.at[step])

    def relax(step, carry):
        start = pl.multiple_of(step * group, group)

        def load(row):
            if row < PASSES:
                ref, at = edge_ref, row
            elif row < PASSES + rows:
                ref, at = field_ref, row - PASSES
            else:
                ref, at = edge_ref, row - rows
            return [ref[at, pl.ds(start, group), piece * LANES : (piece + 1) * LANES] for piece in range(pieces)]

        def renew(planes, done, at):
            above, center, below = planes[at - 1 : at + 2]
            row = at + done
            to_right = [pltpu.roll(piece, 1, 1) for piece in center]
            to_left = [pltpu.roll(piece, LANES - 1, 1) for piece in center]
            fresh = []
            for piece in range(pieces):
                left = jnp.where(at_left, to_right[piece - 1] if piece > 0 else nothing, to_right[piece])
                right = jnp.where(at_right, to_left[piece + 1] if piece < pieces - 1 else nothing, to_left[piece])
                beside = (above[piece] + below[piece]) + (left + right)
                lanes = slice(piece * LANES, (piece + 1) * LANES)
                fresh.append(keep_ref[row, :, lanes] * center[piece] + weight_ref[row, :, lanes] * beside)
            return fresh

        masks = [act_ref[tile, pl.ds(start, group), :] for tile in range(tiles)]
        planes = [load(row) for row in range(total)]
        for done in range(PASSES):
            planes = [renew(planes, done, at) for at in range(1, len(planes) - 1)]
        for own in range(rows):
            for piece in range(pieces):
                at = pl.ds(step * size + piece * rows + own, group, stride=rows * pieces)
                done_ref[at, :] = planes[own][piece] * masks[own // TILE]
        copy(step).start()
        return carry

    lax.fori_loop(0, comps // group, relax, 0, unroll=4)
    for step in range(comps // group):
        copy(step).wait()


def diffuse(where, more, act, correlation, field, inner, outer, outer_again):
    rows, comps, cols = field.shape
    pieces = cols // LANES
    lines = VMEM((rows + 2 * PASSES, GROUP, cols), jnp.float32)
    shape = (comps * rows * pieces, LANES)
    return pl.pallas_call(
        diffuse_kernel,
        name="diffuse",
        in_specs=[SCALARS] * 2 + [WHOLE] * 6,
        out_specs=pl.BlockSpec(memory_space=pltpu.HBM),
        out_shape=jax.ShapeDtypeStruct(shape, jnp.float32),
        scratch_shapes=[
            VMEM(shape, jnp.float32),
            VMEM((2 * PASSES, comps, cols), jnp.float32),
            lines,
            lines,
            pltpu.SemaphoreType.DMA((comps // GROUP,)),
        ],
        compiler_params=pltpu.CompilerParams(vmem_limit_bytes=8 << 20),
    )(where, more, act, correlation, field, inner, outer, outer_again)


def pairs_of(count, first):
    table = list(range(count))
    for i in range(first, count - 1, 2):
        table[i], table[i + 1] = i + 1, i
    return list(enumerate(table))


NEAR, FAR = pairs_of(4, 0), [(0, 3), (1, 2), (2, 1), (3, 0)]


def in_order(odd, mine, other):
    return jnp.concatenate([jnp.where(odd, other, mine), jnp.where(odd, mine, other)], axis=0)


def per_device(recording, traces, footprints, correlation, support):
    comps, rows, cols = footprints.shape
    tiles = rows // TILE
    index = lax.axis_index("rows")
    count = lax.axis_size("rows")
    part = lax.axis_index("tm")
    line = lax.axis_size("tm") == 4
    odd = ((part == 1) | (part == 2)) & line
    where = jnp.stack([index, odd.astype(jnp.int32), jnp.int32(count - 1)]).astype(jnp.int32)
    inside, outside = pairs_of(count, 0), pairs_of(count, 1)
    names = support.T
    field_tiles = tiles_of(footprints)
    spare = comps * tiles - sum(CHUNKS)

    def near(array):
        return lax.ppermute(array, "tm", NEAR)

    def far(array):
        return lax.ppermute(array, "tm", FAR)

    def beside(array):
        return lax.ppermute(array, "rows", outside)

    mine, other = [None, None], [None, None]
    mine[0], other[0] = project(where, names, traces, recording, 0, CHUNKS[:1])
    if not line:
        mine[1], other[1] = project(where, names, traces, recording, CHUNKS[0], CHUNKS[1:])
    *_, later = barrier(other[0], field_tiles)
    planes, act, first, pick, late, more = plan(where, support, later, rows, count)
    if line:
        first_received = near(other[0])
        half = [barrier(mine[0] + first_received, planes)[0]]
        first_across = far(half[0])
        *_, later = barrier(half[0], traces)
        mine[1], other[1] = project(where, names, later, recording, CHUNKS[0], CHUNKS[1:])
        half.append(barrier(mine[1] + near(other[1]))[0])
        whole = [barrier(half[0] + first_across)[0]]
        half[1], whole[0] = barrier(half[1], whole[0])
        first_back = near(whole[0])
        whole.append(barrier(half[1] + far(half[1]))[0])
        back = [first_back, near(whole[1])]
    else:
        whole, back = lax.psum((mine, other), "tm")
    sums = [barrier(in_order(odd, *barrier(whole[0], back[0])))[0]]
    to_outer = edge_rows(where, sums[0], planes, act, first, correlation)
    outer = beside(to_outer)
    *_, later = barrier(to_outer, planes)
    own, theirs, base, rate = barrier(whole[1], back[1], *prepare(sums[0], later, act))
    prepared = base, pick, late, rate
    sums.append(barrier(in_order(odd, own, theirs))[0])

    def rest():
        mine, other = project(where, names, traces, recording, sum(CHUNKS), (spare,))
        if line:
            half = mine + near(other)
            mine = half + far(half)
            other = near(mine)
        else:
            mine, other = lax.psum((mine, other), "tm")
        field, to_inner, to_outer = step_rows(where, prepared, correlation, sums + [in_order(odd, mine, other)])
        return tuple(jnp.maximum(array, 0.0) for array in (field, to_inner, beside(to_outer)))

    def enough():
        return tuple(step_rows(where, prepared, correlation, sums))

    field, to_inner, outer_again = lax.cond(more[0] > 0, rest, enough)
    to_inner, outer = barrier(to_inner, outer)
    inner = lax.ppermute(to_inner, "rows", inside)
    result = diffuse(where, more, act, correlation, field, inner, outer, outer_again)
    return from_tiles(result, comps, rows, cols)


def solution(mesh):
    return jax.shard_map(
        per_device,
        mesh=mesh,
        in_specs=(
            P("tm", ("band", "rows"), None),
            P("band", "tm"),
            P(None, ("band", "rows"), None),
            P(("band", "rows"), None),
            P("band", None),
        ),
        out_specs=P(None, ("band", "rows"), None),
        check_vma=False,
    )
```
